256 devices in a mesh: chan: 64 (over z_lo, y, x), tm: 4 (over z_hi, core).
Axes of the slice: x: 4, y: 4, z: 8 (z_hi: 2, z_lo: 4; z = z_hi * 4 + z_lo), core: 2. Of those that a mesh axis runs over, the one named last changes fastest.
Arguments:
- spectra: bfloat16 [2, 32, 2048, 1024], P(None, 'tm', 'chan'), may hold values from -150 to 150
- quality: int32 [32, 1024], P('tm'), may hold values 0 or 1
- offsets: int32 [4], replicated, may hold values from 1 to 32, as said below
Outputs:
- gathers: float32 [1024, 4, 256], P('chan')
The draws below stay inside these ranges and needn't reach their ends.
Inputs may be any that keep to these rules, and one draw needn't show every extreme that they name: `offsets`: each offset lies from 1 to 32, and one of them equals 32.
All inputs are finite; a program needn't handle non-finite values. No bound on the sum of `quality` on one device may be relied on, other than what follows from the above.
Results may differ from the reference program's by a relative error of at most 0.0003.
Values may be sent and summed in bfloat16 or wider, within the bound.
A program may use at most 64 MiB of HBM per device.

```python
import math
import jax
import jax.numpy as jnp
from jax import lax

F = 2048
LAGS = 256
NOFF = 4
CH_DEV = 16
NCH = 1024
WINDOWS = 32
N_CHAN = 64


def draw_offsets(key, part):
    half_count = N_CHAN // 2
    others = jax.random.randint(jax.random.fold_in(key, 11), (NOFF - 1,), 1, half_count + 1).astype(jnp.int32)
    values = jnp.concatenate([jnp.full((1,), half_count, dtype=jnp.int32), others])
    return jax.random.permutation(jax.random.fold_in(key, 12), values)


def draw_spectra(key, part):
    subkeys = [jax.random.fold_in(key, 21 + number) for number in range(6)]
    chan_pos = jnp.arange(NCH, dtype=jnp.float32)
    freq_pos = jnp.arange(F, dtype=jnp.float32)
    chan_gain = jnp.exp(jax.random.uniform(subkeys[0], (NCH,), minval=0.0, maxval=math.log(10.0)))
    rough_gain = jnp.exp(jax.random.uniform(subkeys[1], (F,), minval=-0.7, maxval=0.7))
    tilt_rate = math.log(3.0)
    noise_part = jax.random.normal(subkeys[4], (2, WINDOWS, F, NCH))
    freq_gain = jnp.exp(tilt_rate * freq_pos / F) * rough_gain
    slowness = jax.random.uniform(subkeys[2], (), minval=0.02, maxval=0.1)
    phase = math.pi * freq_pos[:, None] * (chan_pos[None, :] * slowness) / F
    cosine = jnp.cos(phase)
    sine = jnp.sin(phase)
    source = jax.random.normal(subkeys[3], (2, WINDOWS, F, 1))
    coherent = jnp.stack([source[0] * cosine - source[1] * sine, source[0] * sine + source[1] * cosine])
    values = (coherent + noise_part) * freq_gain[None, None, :, None] * chan_gain[None, None, None, :]
    return jnp.clip(values, -150.0, 150.0).astype(jnp.bfloat16)


def plant(drawn, rng, smallest, top_value):
    dims = drawn.shape
    spot = [jax.random.randint(jax.random.fold_in(rng, axis), (), 0, dims[axis]) for axis in range(len(dims))]
    drawn = drawn.at[tuple(spot)].set(smallest)
    longest = dims.index(max(dims))
    spot[longest] = (spot[longest] + 1) % dims[longest]
    return drawn.at[tuple(spot)].set(top_value)


def setup_inputs(seed: int = 0) -> dict:
    streams_of = jax.random.split(jax.random.key(seed), 4)
    return {
        "spectra": draw_spectra(jax.random.fold_in(streams_of[3], 71), 0),
        "quality": plant((jax.random.randint(streams_of[1], (WINDOWS, NCH), 0, 8) < 7).astype(jnp.int32), jax.random.fold_in(streams_of[1], 1), 0, 1),
        "offsets": draw_offsets(jax.random.fold_in(streams_of[3], 71), 0),
    }


def lag_table(freq_count, lag_count):
    freq_index = jnp.arange(freq_count, dtype=jnp.int32)[:, None]
    double_lag = (2 * jnp.arange(lag_count, dtype=jnp.int32) - lag_count + 1)[None, :]
    turns = jnp.mod(freq_index * double_lag, 4 * freq_count)
    angles = turns.astype(jnp.float32) * (2.0 * math.pi / (4 * freq_count))
    cosine = jnp.cos(angles)
    sine = jnp.sin(angles)
    upper = jnp.concatenate([cosine, sine], axis=1)
    lower = jnp.concatenate([-sine, cosine], axis=1)
    return jnp.stack([upper, lower]).astype(jnp.bfloat16)

def whiten_parts(real_part, imag_part, magnitude, channel_level, usable):
    factor = usable.astype(jnp.float32)[:, None, :] / (magnitude + 0.5 * (channel_level + 1e-05))
    return jnp.stack([real_part * factor, imag_part * factor]).astype(jnp.bfloat16)

def cross_parts(own_real, own_imag, far_real, far_imag):
    own_real = own_real.astype(jnp.float32)
    own_imag = own_imag.astype(jnp.float32)
    far_real = far_real.astype(jnp.float32)
    far_imag = far_imag.astype(jnp.float32)
    return jnp.stack([own_real * far_real + own_imag * far_imag, own_imag * far_real - own_real * far_imag]).astype(jnp.bfloat16)

def pair_terms(corr_all):
    lag_count = corr_all.shape[-1] // 2
    real_corr = corr_all[..., :lag_count]
    imag_corr = corr_all[..., lag_count:]
    power = real_corr * real_corr + imag_corr * imag_corr
    mean_power = lax.optimization_barrier(jnp.mean(power, axis=-1, keepdims=True))
    denominator = jnp.sqrt(power + 0.25 * (mean_power + 1e-06))
    return (lax.optimization_barrier(jnp.sum(real_corr, axis=-3)), lax.optimization_barrier(jnp.sum(real_corr / denominator, axis=-3)), lax.optimization_barrier(jnp.sum(imag_corr / denominator, axis=-3)))

def reference(spectra, quality, offsets):
    real_part = spectra[0].astype(jnp.float32)
    imag_part = spectra[1].astype(jnp.float32)
    magnitude = jnp.sqrt(real_part * real_part + imag_part * imag_part)
    channel_level = lax.optimization_barrier(jnp.sum(magnitude, axis=1, keepdims=True)) / F
    whitened = whiten_parts(real_part, imag_part, magnitude, channel_level, quality)
    padded = jnp.pad(whitened, ((0, 0), (0, 0), (0, 0), (0, NCH)))
    table_wide = lag_table(F, LAGS).astype(jnp.float32)
    inv_root = 1.0 / math.sqrt(F)
    per_offset = []
    for offset_index in range(NOFF):
        shift_cells = (offsets[offset_index] * CH_DEV).astype(jnp.int32)

        def one_block(block, shift_cells=shift_cells):
            start = (block * CH_DEV).astype(jnp.int32)
            own = lax.dynamic_slice_in_dim(whitened, start, CH_DEV, 3)
            partner = lax.dynamic_slice_in_dim(padded, (start + shift_cells).astype(jnp.int32), CH_DEV, 3)
            crossed = cross_parts(own[0], own[1], partner[0], partner[1])
            corr_all = jnp.einsum('cwfh,cfl->whl', crossed.astype(jnp.float32), table_wide) * inv_root
            linear, real_phase, imag_phase = pair_terms(corr_all)
            linear = linear / WINDOWS
            real_phase = real_phase / WINDOWS
            imag_phase = imag_phase / WINDOWS
            return linear * (real_phase * real_phase + imag_phase * imag_phase)
        blocks = lax.map(one_block, jnp.arange(N_CHAN, dtype=jnp.int32))
        per_offset.append(blocks.reshape(NCH, LAGS))
    stacks = jnp.stack(per_offset, axis=1)
    shifted = jnp.pad(stacks, ((NCH, 0), (0, 0), (0, 0)))
    reverse_list = []
    for offset_index in range(NOFF):
        start = (NCH - offsets[offset_index] * CH_DEV).astype(jnp.int32)
        piece = lax.dynamic_slice_in_dim(shifted[:, offset_index], start, NCH, 0)
        reverse_list.append(jnp.flip(piece, axis=1))
    return stacks + jnp.stack(reverse_list, axis=1)
```

```python
import math

import jax
import jax.numpy as jnp
import numpy as np
from jax import lax
from jax.experimental import pallas as pl
from jax.experimental.pallas import tpu as pltpu
from jax.sharding import PartitionSpec as P

MESH = pl.DeviceIdType.MESH
F = 2048
LAGS = 256
HALF = 128
NOFF = 4
WINDOWS = 32
NCH = 1024
TILE = 128
NEED = 5
FB = 32
BF = jnp.bfloat16
F32 = jnp.float32


def place():
    chan = lax.axis_index("chan")
    tm = lax.axis_index("tm")
    return chan // 16, (chan // 4) % 4, chan % 4, tm // 2, tm % 2


def half_table():
    freq = np.arange(F, dtype=np.int64)[None, :]
    lag = 2 * np.arange(HALF, dtype=np.int64)[:, None] + 1
    angle = ((freq * lag) % (4 * F)).astype(np.float64) * (2.0 * math.pi / (4 * F))
    return np.concatenate([np.cos(angle), np.sin(angle)]).astype(np.float32)


def gather_kernel(spec_ref, qual_ref, g_ref, q_ref, send_sem, recv_sem, qsem):
    z, y, x, zh, core = place()
    chan = z * 16 + y * 4 + x
    sib = zh * 2 + 1 - core
    tm = zh * 2 + core
    par = (core + x + 1 + x // 2) % 2
    up = z * 16 + ((y + 1) % 4) * 4 + x
    down = z * 16 + ((y + 3) % 4) * 4 + x

    barrier = pltpu.get_barrier_semaphore()
    spots = [(dz, xh) for dz in (0, 1, 3, 2) for xh in (0, 1)]

    def source(spot):
        return (z + spot[0]) % 4 * 16 + 2 * spot[1] + par

    for spot in spots:
        pl.semaphore_signal(
            barrier, inc=1, device_id=(source(spot) + y * 4, zh * 2 + x // 2), device_id_type=MESH
        )
    for there in ((up, tm), (down, tm), (chan, sib)):
        pl.semaphore_signal(barrier, inc=1, device_id=there, device_id_type=MESH)
    pl.semaphore_wait(barrier, 11)

    started = []

    def forward(block, there):
        copy = pltpu.make_async_remote_copy(
            src_ref=g_ref.at[block],
            dst_ref=g_ref.at[block],
            send_sem=send_sem.at[len(started)],
            recv_sem=recv_sem.at[block],
            device_id=there,
            device_id_type=MESH,
        )
        copy.start()
        started.append(copy)

    def arrive(block):
        pltpu.make_async_remote_copy(
            src_ref=g_ref.at[block],
            dst_ref=g_ref.at[block],
            send_sem=send_sem.at[0],
            recv_sem=recv_sem.at[block],
            device_id=(chan, sib),
            device_id_type=MESH,
        ).wait_recv()

    for dz, low in spots:
        zt = (z + dz) % 4
        copy = pltpu.make_async_remote_copy(
            src_ref=spec_ref.at[:, 2 * zt + low],
            dst_ref=g_ref.at[chan],
            send_sem=send_sem.at[len(started)],
            recv_sem=recv_sem.at[chan],
            device_id=(zt * 16 + y * 4 + low + 2 * core, zh * 2 + (x + low + 1 + core) % 2),
            device_id_type=MESH,
        )
        copy.start()
        started.append(copy)
    qcopy = pltpu.make_async_remote_copy(
        src_ref=qual_ref,
        dst_ref=q_ref,
        send_sem=qsem.at[0],
        recv_sem=qsem.at[1],
        device_id=(chan, sib),
        device_id_type=MESH,
    )
    qcopy.start()

    def own(n):
        block = source(spots[n]) + y * 4
        arrive(block)
        forward(block, (up, tm))
        forward(block, (down, tm))
        forward(block, (chan, sib))

    def near(n):
        block = source(spots[n]) + (y + 3) % 4 * 4
        arrive(block)
        if n < 4:
            forward(block, (up, tm))
        forward(block, (chan, sib))
        block = source(spots[n]) + (y + 1) % 4 * 4
        arrive(block)
        if n >= 4:
            forward(block, (down, tm))
        forward(block, (chan, sib))

    def far(n):
        block = source(spots[n]) + (y + 2) % 4 * 4
        arrive(block)
        forward(block, (chan, sib))

    for n in range(10):
        if n < 8:
            own(n)
        if 0 <= n - 1 < 8:
            near(n - 1)
        if 0 <= n - 2 < 8:
            far(n - 2)
    for n in range(8):
        for dy in range(4):
            zs = (z + spots[n][0]) % 4
            arrive(zs * 16 + (y + dy) % 4 * 4 + 2 * spots[n][1] + 1 - par)
    qcopy.wait()
    for copy in started:
        copy.wait_send()


def gather_window(spectra, quality):
    any_spec = pl.BlockSpec(memory_space=pl.ANY)
    return pl.pallas_call(
        gather_kernel,
        name="gather_window",
        out_shape=(
            jax.ShapeDtypeStruct((64, 2, FB, NCH), BF),
            jax.ShapeDtypeStruct((8, NCH), jnp.int32),
        ),
        in_specs=[any_spec, any_spec],
        out_specs=(any_spec, any_spec),
        scratch_shapes=[
            pltpu.SemaphoreType.DMA((64,)),
            pltpu.SemaphoreType.DMA((64,)),
            pltpu.SemaphoreType.DMA((2,)),
        ],
        compiler_params=pltpu.CompilerParams(collective_id=0, has_side_effects=True),
    )(spectra, quality)


def corr_kernel(sc_ref, g_ref, qual_ref, tab_ref, out_ref, w_ref, mag_ref, acc_ref, x_ref):
    step = pl.program_id(0)

    @pl.when(step < NEED)
    def _():
        def measure(n, total):
            re = g_ref[n, 0].astype(F32)
            im = g_ref[n, 1].astype(F32)
            mag = jnp.sqrt(re * re + im * im)
            mag_ref[n] = mag
            return total + mag

        total = lax.fori_loop(0, 64, measure, jnp.zeros((FB, TILE), F32), unroll=4)
        level = jnp.sum(total, axis=0, keepdims=True) / F
        add = 0.5 * (level + 1e-05)
        live = jnp.where(sc_ref[0] + step < 8, 1.0, 0.0).astype(F32)
        usable = qual_ref[0:1, :].astype(F32) * live

        def whiten(n, carry):
            factor = usable / (mag_ref[n] + add)
            w_ref[step, 0, n] = (g_ref[n, 0].astype(F32) * factor).astype(BF)
            w_ref[step, 1, n] = (g_ref[n, 1].astype(F32) * factor).astype(BF)
            return carry

        lax.fori_loop(0, 64, whiten, 0, unroll=4)

    @pl.when(step == NEED)
    def _():
        lane = lax.broadcasted_iota(jnp.int32, (256, TILE), 1)
        for n in range(8):
            rows = pl.ds(8 * n, 8)

            def grab(tile, part, rows=rows):
                return w_ref[tile, part, rows].astype(F32).reshape(256, TILE)

            own_re = grab(0, 0)
            own_im = grab(0, 1)
            for j in range(NOFF):
                whole = sc_ref[1 + j] // 8
                rest = sc_ref[1 + j] % 8 * 16
                keep = lane >= rest
                back = (TILE - rest) % TILE
                far_re = pltpu.roll(jnp.where(keep, grab(whole, 0), grab(whole + 1, 0)), back, 1)
                far_im = pltpu.roll(jnp.where(keep, grab(whole, 1), grab(whole + 1, 1)), back, 1)
                x_ref[:, j * TILE : (j + 1) * TILE] = (own_re * far_re + own_im * far_im).astype(BF)
                x_ref[:, 512 + j * TILE : 512 + (j + 1) * TILE] = (own_im * far_re - own_re * far_im).astype(BF)
            part = jnp.dot(tab_ref[:, 256 * n : 256 * (n + 1)], x_ref[...], preferred_element_type=F32)
            if n == 0:
                acc_ref[...] = part
            else:
                acc_ref[...] += part
        scale = 1.0 / math.sqrt(F)
        for j in range(NOFF):
            left = slice(j * TILE, (j + 1) * TILE)
            right = slice(512 + j * TILE, 512 + (j + 1) * TILE)
            a = acc_ref[:HALF, left]
            b = acc_ref[HALF:, right]
            c = acc_ref[HALF:, left]
            d = acc_ref[:HALF, right]
            pos_r = (a - b) * scale
            neg_r = (a + b) * scale
            pos_q = (d + c) * scale
            neg_q = (d - c) * scale
            pos_p = pos_r * pos_r + pos_q * pos_q
            neg_p = neg_r * neg_r + neg_q * neg_q
            mean = jnp.sum(pos_p + neg_p, axis=0, keepdims=True) / LAGS
            floor = 0.25 * (mean + 1e-06)
            pos_d = jnp.sqrt(pos_p + floor)
            neg_d = jnp.sqrt(neg_p + floor)
            out_ref[0, 0, :, left] = pos_r
            out_ref[0, 1, :, left] = neg_r
            out_ref[1, 0, :, left] = pos_r / pos_d
            out_ref[1, 1, :, left] = neg_r / neg_d
            out_ref[2, 0, :, left] = pos_q / pos_d
            out_ref[2, 1, :, left] = neg_q / neg_d


def correlate(scalars, gathered, usable, table):
    grid_spec = pltpu.PrefetchScalarGridSpec(
        num_scalar_prefetch=1,
        grid=(NEED + 1,),
        in_specs=[
            pl.BlockSpec((64, 2, FB, TILE), lambda s, sc: (0, 0, 0, jnp.minimum(sc[0] + jnp.minimum(s, NEED - 1), 7))),
            pl.BlockSpec((8, TILE), lambda s, sc: (0, jnp.minimum(sc[0] + jnp.minimum(s, NEED - 1), 7))),
            pl.BlockSpec((2 * HALF, F), lambda s, sc: (0, 0)),
        ],
        out_specs=pl.BlockSpec((3, 2, HALF, NOFF * TILE), lambda s, sc: (0, 0, 0, 0)),
        scratch_shapes=[
            pltpu.VMEM((NEED + 1, 2, 64, FB, TILE), BF),
            pltpu.VMEM((64, FB, TILE), F32),
            pltpu.VMEM((2 * HALF, 2 * NOFF * TILE), F32),
            pltpu.VMEM((256, 2 * NOFF * TILE), BF),
        ],
    )
    return pl.pallas_call(
        corr_kernel,
        name="correlate",
        grid_spec=grid_spec,
        out_shape=jax.ShapeDtypeStruct((3, 2, HALF, NOFF * TILE), F32),
    )(scalars, gathered, usable, table)


def tail_kernel(off_ref, p_ref, out_ref, xbuf, zacc, zbuf, st, tbuf, jbuf, mbuf, rbuf, send_sem, recv_sem):
    zl, y, x, zh, core = place()
    chan = zl * 16 + y * 4 + x
    tm = zh * 2 + core
    z = zh * 4 + zl
    t = y * 2 + core

    def x_peer(d):
        return (zl * 16 + y * 4 + (x + d) % 4, tm)

    def z_peer(d):
        there = (z + d) % 8
        return (there % 4 * 16 + y * 4 + x, there // 4 * 2 + core)

    def t_peer(d):
        there = (t + d) % 8
        return (zl * 16 + there // 2 * 4 + x, zh * 2 + there % 2)

    barrier = pltpu.get_barrier_semaphore()
    peers = [x_peer(d) for d in (1, 2, 3)] + [z_peer(d) for d in range(1, 8)] + [t_peer(d) for d in range(1, 8)]
    for there in peers:
        pl.semaphore_signal(barrier, inc=1, device_id=there, device_id_type=MESH)
    pl.semaphore_wait(barrier, len(peers))

    started = []

    def send(src, dst, there):
        copy = pltpu.make_async_remote_copy(
            src_ref=src,
            dst_ref=dst,
            send_sem=send_sem.at[len(started)],
            recv_sem=recv_sem.at[len(started)],
            device_id=there,
            device_id_type=MESH,
        )
        copy.start()
        started.append(copy)
        return copy

    def columns(where):
        return pl.ds(pl.multiple_of(where * TILE, TILE), TILE)

    copies = [
        send(p_ref.at[:, :, :, columns((x + d) % 4)], xbuf.at[d - 1], x_peer(d)) for d in (1, 2, 3)
    ]
    for copy in copies:
        copy.wait_recv()
    mine = p_ref[:, :, :, columns(x)]
    zacc[...] = (mine + xbuf[0]) + (xbuf[1] + xbuf[2])

    def lag_rows(where):
        return pl.ds(pl.multiple_of(where * 16, 16), 16)

    copies = [
        send(zacc.at[:, :, lag_rows((z + d) % 8)], zbuf.at[d - 1], z_peer(d)) for d in range(1, 8)
    ]
    total = zacc[:, :, lag_rows(z)]
    for d, copy in enumerate(copies):
        copy.wait_recv()
        total = total + zbuf[d]
    linear = total[0] / WINDOWS
    real = total[1] / WINDOWS
    imag = total[2] / WINDOWS
    st[t] = linear * (real * real + imag * imag)

    copies = [send(st.at[t], st.at[t], t_peer(d)) for d in range(1, 8)]
    for copy in copies:
        copy.wait_recv()
    shift = off_ref[x]
    whole = shift // 8
    rest = shift % 8 * 16
    lane = lax.broadcasted_iota(jnp.int32, (2, 16, TILE), 2)
    pieces = []
    for n in range(4):
        tile = 2 * n + y // 2
        first = tile - whole
        a = jnp.where(first >= 0, st[jnp.maximum(first, 0)], 0.0)
        b = jnp.where(first >= 1, st[jnp.maximum(first - 1, 0)], 0.0)
        rev = pltpu.roll(jnp.where(lane < TILE - rest, a, b).reshape(32, TILE), rest, 1).reshape(2, 16, TILE)
        ahead = st[tile]
        pieces.append(ahead[0] + rev[1])
        pieces.append(ahead[1] + rev[0])
    tbuf[...] = jnp.concatenate(pieces, axis=0).T

    def channel_rows(where):
        return pl.ds(pl.multiple_of(y % 2 * 64 + where * 16, 16), 16)

    copies = [send(tbuf.at[channel_rows((x + d) % 4)], jbuf.at[x], x_peer(d)) for d in (1, 2, 3)]
    jbuf[x] = tbuf[channel_rows(x)]
    for copy in copies:
        copy.wait_recv()
    group = lax.broadcasted_iota(jnp.int32, (16, TILE), 1) // 32
    for n in range(4):
        merged = jnp.zeros((16, TILE), F32)
        for j in range(NOFF):
            merged = jnp.where(group == j, pltpu.roll(jbuf[j], (32 * (j - n)) % TILE, 1), merged)
        mbuf[n] = merged
    copies = [send(mbuf.at[(z + d) % 4], rbuf.at[z], z_peer(d)) for d in range(1, 8)]
    rbuf[z] = mbuf[z % 4]
    for copy in copies:
        copy.wait_recv()
    span = lax.broadcasted_iota(jnp.int32, (16, TILE), 1) // 16
    for j in range(NOFF):
        for s in range(2):
            merged = jnp.zeros((16, TILE), F32)
            for n in range(8):
                merged = jnp.where(span == n, pltpu.roll(rbuf[n], (16 * n - 32 * j - 16 * s) % TILE, 1), merged)
            out_ref[j, s] = merged
    for copy in started:
        copy.wait_send()


def finish(offsets, sums):
    count = 3 + 7 + 7 + 3 + 7
    vmem = pl.BlockSpec(memory_space=pltpu.VMEM)
    return pl.pallas_call(
        tail_kernel,
        name="finish",
        out_shape=jax.ShapeDtypeStruct((NOFF, 2, 16, TILE), F32),
        in_specs=[pl.BlockSpec(memory_space=pltpu.SMEM), vmem],
        out_specs=vmem,
        scratch_shapes=[
            pltpu.VMEM((3, 3, 2, HALF, TILE), F32),
            pltpu.VMEM((3, 2, HALF, TILE), F32),
            pltpu.VMEM((7, 3, 2, 16, TILE), F32),
            pltpu.VMEM((8, 2, 16, TILE), F32),
            pltpu.VMEM((TILE, TILE), F32),
            pltpu.VMEM((NOFF, 16, TILE), F32),
            pltpu.VMEM((4, 16, TILE), F32),
            pltpu.VMEM((8, 16, TILE), F32),
            pltpu.SemaphoreType.DMA((count,)),
            pltpu.SemaphoreType.DMA((count,)),
        ],
        compiler_params=pltpu.CompilerParams(collective_id=1, has_side_effects=True),
    )(offsets, sums)


def shards(spectra, quality, offsets):
    z, y, x, zh, core = place()
    gathered, other = gather_window(spectra, quality)
    mine = jnp.where(x // 2 == core, quality, other)
    usable = lax.dynamic_slice_in_dim(mine, 2 * z + x % 2, 1, 0)
    usable = jnp.broadcast_to(usable, (8, NCH))
    table = jnp.asarray(half_table()).astype(BF)
    scalars = jnp.concatenate([(y * 2 + core).astype(jnp.int32)[None], offsets.astype(jnp.int32)])
    sums = correlate(scalars, gathered, usable, table)
    halves = finish(offsets, sums)
    late = jnp.transpose(halves[:, 0], (1, 0, 2))
    early = jnp.flip(jnp.transpose(halves[:, 1], (1, 0, 2)), axis=2)
    return jnp.concatenate([early, late], axis=2)


def solution(mesh):
    return jax.shard_map(
        shards,
        mesh=mesh,
        in_specs=(P(None, "tm", "chan", None), P("tm", None), P()),
        out_specs=P("chan", None, None),
        check_vma=False,
    )
```

```python
import math

import jax
import jax.numpy as jnp
import numpy as np
from jax import lax
from jax.experimental import pallas as pl
from jax.experimental.pallas import tpu as pltpu
from jax.sharding import PartitionSpec as P

MESH = pl.DeviceIdType.MESH
F = 2048
LAGS = 256
HALF = 128
NOFF = 4
WINDOWS = 32
NCH = 1024
TILE = 128
NEED = 5
FB = 32
GROUP = 256
BF = jnp.bfloat16
F32 = jnp.float32


def place():
    chan = lax.axis_index("chan")
    tm = lax.axis_index("tm")
    return chan // 16, (chan // 4) % 4, chan % 4, tm // 2, tm % 2


def half_table():
    y, par, z, half, low = np.meshgrid(*(np.arange(n) for n in (4, 2, 4, 2, FB)), indexing="ij")
    freq = ((z * 16 + y * 4 + 2 * half + par) * FB + low).reshape(8, 1, GROUP).astype(np.int64)
    lag = (2 * np.arange(HALF, dtype=np.int64) + 1)[None, :, None]
    angle = ((freq * lag) % (4 * F)).astype(np.float64) * (2.0 * math.pi / (4 * F))
    return np.concatenate([np.cos(angle), np.sin(angle)], axis=1).astype(np.float32)


def tile_at(where):
    return pl.ds(pl.multiple_of(where * TILE, TILE), TILE)


def window_kernel(
    off_ref, spec_ref, qual_ref, tab_ref, out_ref,
    g, qbuf, lvall, add_ref, use_ref, w, xmat, acc, p,
    ring, ringsum, ringin, zacc, zbuf, st, tbuf, jbuf, mbuf, rbuf,
    gsend, grecv, send_sem, recv_sem,
):
    z, y, x, zh, core = place()
    chan = z * 16 + y * 4 + x
    tm = zh * 2 + core
    sib = (chan, zh * 2 + 1 - core)
    t = y * 2 + core
    zall = zh * 4 + z
    par = (core + x + 1 + x // 2) % 2
    up = (z * 16 + ((y + 1) % 4) * 4 + x, tm)
    down = (z * 16 + ((y + 3) % 4) * 4 + x, tm)

    def x_peer(d):
        return (z * 16 + y * 4 + (x + d) % 4, tm)

    def z_peer(d):
        there = (zall + d) % 8
        return (there % 4 * 16 + y * 4 + x, there // 4 * 2 + core)

    def t_peer(d):
        there = (t + d) % 8
        return (z * 16 + there // 2 * 4 + x, zh * 2 + there % 2)

    mate = z + 1 - 2 * (z % 2)
    zs = [z, mate, 3 - z, 3 - mate]
    spots = [(zs[k], xh) for k in range(4) for xh in (0, 1)]

    barrier = pltpu.get_barrier_semaphore()
    greet = [(zt * 16 + y * 4 + 2 * xh + par, zh * 2 + x // 2) for zt, xh in spots]
    greet += [x_peer(d) for d in (1, 2, 3)]
    greet += [z_peer(d) for d in range(1, 8)]
    greet += [t_peer(d) for d in range(1, 8)]
    for there in greet:
        pl.semaphore_signal(barrier, inc=1, device_id=there, device_id_type=MESH)
    pl.semaphore_wait(barrier, len(greet))

    sent = []
    started = []

    def put(src, where, there):
        copy = pltpu.make_async_remote_copy(
            src_ref=src,
            dst_ref=g.at[where[0], where[1]],
            send_sem=gsend.at[len(sent)],
            recv_sem=grecv.at[where[0], where[1]],
            device_id=there,
            device_id_type=MESH,
        )
        copy.start()
        sent.append(len(sent))

    def forward(where, there):
        put(g.at[where[0], where[1]], where, there)

    def arrive(where):
        pltpu.make_async_remote_copy(
            src_ref=g.at[where[0], where[1]],
            dst_ref=g.at[where[0], where[1]],
            send_sem=gsend.at[0],
            recv_sem=grecv.at[where[0], where[1]],
            device_id=sib,
            device_id_type=MESH,
        ).wait_recv()

    def send(src, dst, there):
        copy = pltpu.make_async_remote_copy(
            src_ref=src,
            dst_ref=dst,
            send_sem=send_sem.at[len(started)],
            recv_sem=recv_sem.at[len(started)],
            device_id=there,
            device_id_type=MESH,
        )
        copy.start()
        started.append(copy)
        return copy

    home = (y * 2 + x % 2, z * 2 + x // 2)
    for zt, low in spots:
        put(
            spec_ref.at[:, 2 * zt + low],
            home,
            (zt * 16 + y * 4 + low + 2 * core, zh * 2 + (x + low + 1 + core) % 2),
        )
    qcopy = send(qual_ref, qbuf, sib)

    def block(n, dy):
        return ((y + dy) % 4 * 2 + par, spots[n][0] * 2 + spots[n][1])

    def own(n):
        here = block(n, 0)
        arrive(here)
        forward(here, up)
        forward(here, down)
        forward(here, sib)
        re = g[here[0], here[1], 0].astype(F32)
        im = g[here[0], here[1], 1].astype(F32)
        mag = jnp.sqrt(re * re + im * im)
        part = jnp.sum(mag, axis=0, keepdims=True)
        if n == 0:
            lvall[t] = part
        else:
            lvall[t] = lvall[t] + part

    def near(n):
        here = block(n, 3)
        arrive(here)
        if n % 2 == 0:
            forward(here, up)
        forward(here, sib)
        here = block(n, 1)
        arrive(here)
        if n % 2 == 1:
            forward(here, down)
        forward(here, sib)

    def far(n):
        here = block(n, 2)
        arrive(here)
        forward(here, sib)

    for n in range(8):
        own(n)
        if n == 7:
            levels = [send(lvall.at[t], lvall.at[t], t_peer(d)) for d in range(1, 8)]
        if n >= 1:
            near(n - 1)
        if n >= 2:
            far(n - 2)
    qcopy.wait_recv()
    row = pl.ds(2 * z + x % 2, 1)
    use_ref[...] = jnp.where(x // 2 == core, qual_ref[row], qbuf[row]).astype(F32)
    for copy in levels:
        copy.wait_recv()
    level = lvall[0]
    for n in range(1, 8):
        level = level + lvall[n]
    add_ref[...] = 0.5 * (level / F + 1e-05)
    acc[...] = jnp.zeros_like(acc)
    lane = lax.broadcasted_iota(jnp.int32, (FB, TILE), 1)

    def compute(gi):
        def whiten(k, carry):
            for m in range(NEED):
                cols = tile_at(jnp.minimum(t + m, 7))
                live = jnp.where(t + m < 8, 1.0, 0.0)
                re = g[gi, k, 0, :, cols].astype(F32)
                im = g[gi, k, 1, :, cols].astype(F32)
                mag = jnp.sqrt(re * re + im * im)
                factor = (use_ref[:, cols] * live) / (mag + add_ref[:, cols])
                w[m, 0, k] = (re * factor).astype(BF)
                w[m, 1, k] = (im * factor).astype(BF)
            return carry

        lax.fori_loop(0, 8, whiten, 0)

        def cross(k, carry):
            rows = pl.ds(pl.multiple_of(k * FB, FB), FB)
            own_re = w[0, 0, k].astype(F32)
            own_im = w[0, 1, k].astype(F32)
            for j in range(NOFF):
                whole = off_ref[j] // 8
                rest = off_ref[j] % 8 * 16
                keep = lane >= rest
                back = (TILE - rest) % TILE
                far_re = jnp.where(keep, w[whole, 0, k].astype(F32), w[whole + 1, 0, k].astype(F32))
                far_im = jnp.where(keep, w[whole, 1, k].astype(F32), w[whole + 1, 1, k].astype(F32))
                far_re = pltpu.roll(far_re, back, 1)
                far_im = pltpu.roll(far_im, back, 1)
                xmat[rows, j * TILE : (j + 1) * TILE] = (own_re * far_re + own_im * far_im).astype(BF)
                xmat[rows, 512 + j * TILE : 512 + (j + 1) * TILE] = (own_im * far_re - own_re * far_im).astype(BF)
            return carry

        lax.fori_loop(0, 8, cross, 0)
        acc[...] += jnp.dot(tab_ref[gi], xmat[...], preferred_element_type=F32)

    w[NEED] = jnp.zeros_like(w[NEED])

    def turn(i, carry):
        @pl.when(i == 1)
        def _():
            near(7)
            far(6)

        @pl.when(i == 3)
        def _():
            far(7)

        dy = jnp.where(i < 2, 0, jnp.where(i >= 6, 2, jnp.where(i % 2 == 0, 3, 1)))
        other = jnp.where((i == 1) | (i == 4) | (i == 5) | (i == 7), 1, 0)
        gi = (y + dy) % 4 * 2 + (par + other) % 2

        @pl.when(other == 1)
        def _():
            for k in range(8):
                arrive((gi, k))

        compute(gi)
        return carry

    lax.fori_loop(0, 8, turn, 0)

    scale = 1.0 / math.sqrt(F)

    def phases(j):
        left = tile_at(j)
        right = tile_at(j + NOFF)
        a = acc[:HALF, left]
        b = acc[HALF:, right]
        c = acc[HALF:, left]
        d = acc[:HALF, right]
        pos_r = (a - b) * scale
        neg_r = (a + b) * scale
        pos_q = (d + c) * scale
        neg_q = (d - c) * scale
        pos_p = pos_r * pos_r + pos_q * pos_q
        neg_p = neg_r * neg_r + neg_q * neg_q
        mean = jnp.sum(pos_p + neg_p, axis=0, keepdims=True) / LAGS
        floor = 0.25 * (mean + 1e-06)
        pos_d = jnp.sqrt(pos_p + floor)
        neg_d = jnp.sqrt(neg_p + floor)
        p[0, 0, j] = pos_r
        p[1, 0, j] = neg_r
        p[0, 1, j] = pos_r / pos_d
        p[1, 1, j] = neg_r / neg_d
        p[0, 2, j] = pos_q / pos_d
        p[1, 2, j] = neg_q / neg_d

    right, left, across = (x + 1) % 4, (x + 3) % 4, (x + 2) % 4
    phases(across)
    to_right = send(p.at[0, :, across], ring.at[0], x_peer(1))
    to_left = send(p.at[1, :, across], ring.at[1], x_peer(3))
    phases(right)
    plain_right = send(p.at[1, :, right], ringin.at[0], x_peer(1))
    phases(left)
    plain_left = send(p.at[0, :, left], ringin.at[1], x_peer(3))
    phases(x)
    to_right.wait_recv()
    ringsum[0] = ring[0] + p[0, :, right]
    both_right = send(ringsum.at[0], ringin.at[2], x_peer(1))
    to_left.wait_recv()
    ringsum[1] = ring[1] + p[1, :, left]
    both_left = send(ringsum.at[1], ringin.at[3], x_peer(3))
    plain_right.wait_recv()
    plain_left.wait_recv()
    both_right.wait_recv()
    zacc[0] = (p[0, :, x] + ringin[1]) + ringin[2]
    both_left.wait_recv()
    zacc[1] = (p[1, :, x] + ringin[0]) + ringin[3]

    def lag_rows(where):
        return pl.ds(pl.multiple_of(where * 16, 16), 16)

    copies = [
        send(zacc.at[:, :, lag_rows((zall + d) % 8)], zbuf.at[d - 1], z_peer(d)) for d in (4, 3, 5, 2, 6, 1, 7)
    ]
    total = zacc[:, :, lag_rows(zall)]
    for copy in copies:
        copy.wait_recv()
    for d in range(7):
        total = total + zbuf[d]
    linear = total[:, 0] / WINDOWS
    real = total[:, 1] / WINDOWS
    imag = total[:, 2] / WINDOWS
    st[t] = linear * (real * real + imag * imag)

    copies = [send(st.at[t], st.at[t], t_peer(d)) for d in range(1, 8)]
    for copy in copies:
        copy.wait_recv()
    shift = off_ref[x]
    whole = shift // 8
    rest = shift % 8 * 16
    wide = lax.broadcasted_iota(jnp.int32, (2, 16, TILE), 2)
    pieces = []
    for n in range(4):
        tile = 2 * n + y // 2
        first = tile - whole
        a = jnp.where(first >= 0, st[jnp.maximum(first, 0)], 0.0)
        b = jnp.where(first >= 1, st[jnp.maximum(first - 1, 0)], 0.0)
        rev = pltpu.roll(jnp.where(wide < TILE - rest, a, b).reshape(32, TILE), rest, 1).reshape(2, 16, TILE)
        ahead = st[tile]
        pieces.append(ahead[0] + rev[1])
        pieces.append(ahead[1] + rev[0])
    tbuf[...] = jnp.concatenate(pieces, axis=0).T

    def channel_rows(where):
        return pl.ds(pl.multiple_of(y % 2 * 64 + where * 16, 16), 16)

    copies = [send(tbuf.at[channel_rows((x + d) % 4)], jbuf.at[x], x_peer(d)) for d in (1, 2, 3)]
    jbuf[x] = tbuf[channel_rows(x)]
    for copy in copies:
        copy.wait_recv()
    group = lax.broadcasted_iota(jnp.int32, (16, TILE), 1) // 32
    for n in range(4):
        merged = jnp.zeros((16, TILE), F32)
        for j in range(NOFF):
            merged = jnp.where(group == j, pltpu.roll(jbuf[j], (32 * (j - n)) % TILE, 1), merged)
        mbuf[n] = merged
    copies = [send(mbuf.at[(zall + d) % 4], rbuf.at[zall], z_peer(d)) for d in (4, 3, 5, 2, 6, 1, 7)]
    rbuf[zall] = mbuf[zall % 4]
    for copy in copies:
        copy.wait_recv()
    span = lax.broadcasted_iota(jnp.int32, (16, TILE), 1) // 16
    for j in range(NOFF):
        for s in range(2):
            merged = jnp.zeros((16, TILE), F32)
            for n in range(8):
                merged = jnp.where(span == n, pltpu.roll(rbuf[n], (16 * n - 32 * j - 16 * s) % TILE, 1), merged)
            out_ref[j, s] = merged
    for n in sent:
        pltpu.make_async_remote_copy(
            src_ref=g.at[0, 0],
            dst_ref=g.at[0, 0],
            send_sem=gsend.at[n],
            recv_sem=grecv.at[0, 0],
            device_id=sib,
            device_id_type=MESH,
        ).wait_send()
    for copy in started:
        copy.wait_send()


def whole_window(offsets, spectra, quality, table):
    vmem = pl.BlockSpec(memory_space=pltpu.VMEM)
    return pl.pallas_call(
        window_kernel,
        name="whole_window",
        out_shape=jax.ShapeDtypeStruct((NOFF, 2, 16, TILE), F32),
        in_specs=[pl.BlockSpec(memory_space=pltpu.SMEM), pl.BlockSpec(memory_space=pl.ANY), vmem, vmem],
        out_specs=vmem,
        scratch_shapes=[
            pltpu.VMEM((8, 8, 2, FB, NCH), BF),
            pltpu.VMEM((8, NCH), jnp.int32),
            pltpu.VMEM((8, 1, NCH), F32),
            pltpu.VMEM((1, NCH), F32),
            pltpu.VMEM((1, NCH), F32),
            pltpu.VMEM((NEED + 1, 2, 8, FB, TILE), BF),
            pltpu.VMEM((GROUP, 2 * NOFF * TILE), BF),
            pltpu.VMEM((2 * HALF, 2 * NOFF * TILE), F32),
            pltpu.VMEM((2, 3, NOFF, HALF, TILE), F32),
            pltpu.VMEM((2, 3, HALF, TILE), F32),
            pltpu.VMEM((2, 3, HALF, TILE), F32),
            pltpu.VMEM((4, 3, HALF, TILE), F32),
            pltpu.VMEM((2, 3, HALF, TILE), F32),
            pltpu.VMEM((7, 2, 3, 16, TILE), F32),
            pltpu.VMEM((8, 2, 16, TILE), F32),
            pltpu.VMEM((TILE, TILE), F32),
            pltpu.VMEM((NOFF, 16, TILE), F32),
            pltpu.VMEM((4, 16, TILE), F32),
            pltpu.VMEM((8, 16, TILE), F32),
            pltpu.SemaphoreType.DMA((64,)),
            pltpu.SemaphoreType.DMA((8, 8)),
            pltpu.SemaphoreType.DMA((40,)),
            pltpu.SemaphoreType.DMA((40,)),
        ],
        compiler_params=pltpu.CompilerParams(collective_id=0, has_side_effects=True),
    )(offsets, spectra, quality, table)


def shards(spectra, quality, offsets):
    table = jnp.asarray(half_table()).astype(BF)
    halves = whole_window(offsets, spectra, quality, table)
    late = jnp.transpose(halves[:, 0], (1, 0, 2))
    early = jnp.flip(jnp.transpose(halves[:, 1], (1, 0, 2)), axis=2)
    return jnp.concatenate([early, late], axis=2)


def solution(mesh):
    return jax.shard_map(
        shards,
        mesh=mesh,
        in_specs=(P(None, "tm", "chan", None), P("tm", None), P()),
        out_specs=P("chan", None, None),
        check_vma=False,
    )
```

```python
import math

import jax
import jax.numpy as jnp
import numpy as np
from jax import lax
from jax.experimental import pallas as pl
from jax.experimental.pallas import tpu as pltpu
from jax.sharding import PartitionSpec as P

MESH = pl.DeviceIdType.MESH
F = 2048
LAGS = 256
HALF = 128
NOFF = 4
WINDOWS = 32
NCH = 1024
TILE = 128
FB = 32
NEED = 5
GROUP = 256
BF = jnp.bfloat16
F32 = jnp.float32


def place():
    chan = lax.axis_index("chan")
    tm = lax.axis_index("tm")
    return chan // 16, (chan // 4) % 4, chan % 4, tm // 2, tm % 2


def half_table():
    z, half, y, par, low = np.meshgrid(*(np.arange(n) for n in (4, 2, 4, 2, FB)), indexing="ij")
    freq = ((z * 16 + y * 4 + 2 * half + par) * FB + low).reshape(8, 1, GROUP).astype(np.int64)
    lag = (2 * np.arange(HALF, dtype=np.int64) + 1)[None, :, None]
    angle = ((freq * lag) % (4 * F)).astype(np.float64) * (2.0 * math.pi / (4 * F))
    return np.concatenate([np.cos(angle), np.sin(angle)], axis=1).astype(np.float32)


def tile_at(where):
    return pl.ds(pl.multiple_of(where * TILE, TILE), TILE)


def window_kernel(
    off_ref, spec_ref, qual_ref, tab_hbm, out_ref,
    spec, qown, qbuf, tab, g, lvown, lvin, lvall, add_ref, use_ref, w, xmat, acc, p,
    ring, ringsum, ringin, zacc, zbuf, st, tbuf, jbuf, mbuf, rbuf,
    local_sem, own_sem, row_sem, gsend, grecv, send_sem, recv_sem,
):
    z, y, x, zh, core = place()
    chan = z * 16 + y * 4 + x
    tm = zh * 2 + core
    sib = (chan, zh * 2 + 1 - core)
    t = y * 2 + core
    zall = zh * 4 + z
    par = (core + x + 1 + x // 2) % 2
    up = (z * 16 + ((y + 1) % 4) * 4 + x, tm)
    down = (z * 16 + ((y + 3) % 4) * 4 + x, tm)

    def x_peer(d):
        return (z * 16 + y * 4 + (x + d) % 4, tm)

    def z_peer(d):
        there = (zall + d) % 8
        return (there % 4 * 16 + y * 4 + x, there // 4 * 2 + core)

    def t_peer(d):
        there = (t + d) % 8
        return (z * 16 + there // 2 * 4 + x, zh * 2 + there % 2)

    mate = z + 1 - 2 * (z % 2)
    zs = [z, mate, 3 - z, 3 - mate]
    spots = [(zs[k], xh) for k in range(4) for xh in (0, 1)]

    loads = [
        pltpu.make_async_copy(src, dst, local_sem.at[n])
        for n, (src, dst) in enumerate(((spec_ref, spec), (qual_ref, qown), (tab_hbm, tab)))
    ]
    for copy in loads:
        copy.start()
    barrier = pltpu.get_barrier_semaphore()
    greet = [(zt * 16 + y * 4 + 2 * xh + par, zh * 2 + x // 2) for zt, xh in spots]
    greet += [x_peer(d) for d in (1, 2, 3)]
    greet += [z_peer(d) for d in range(1, 8)]
    greet += [t_peer(d) for d in range(1, 8)]
    for there in greet:
        pl.semaphore_signal(barrier, inc=1, device_id=there, device_id_type=MESH)
    loads[0].wait()

    def measure(i, carry):
        re = spec[0, i].astype(F32)
        im = spec[1, i].astype(F32)
        lvown[i] = jnp.sum(jnp.sqrt(re * re + im * im), axis=0, keepdims=True)
        return carry

    lax.fori_loop(0, 8, measure, 0)
    pl.semaphore_wait(barrier, len(greet))

    started = []

    def send(src, dst, there):
        copy = pltpu.make_async_remote_copy(
            src_ref=src,
            dst_ref=dst,
            send_sem=send_sem.at[len(started)],
            recv_sem=recv_sem.at[len(started)],
            device_id=there,
            device_id_type=MESH,
        )
        copy.start()
        started.append(copy)
        return copy

    landings = [
        (2 * zt + low, (zt * 16 + y * 4 + low + 2 * core, zh * 2 + (x + low + 1 + core) % 2)) for zt, low in spots
    ]
    home = z * 2 + x // 2
    first_hop = []
    for n, (i, there) in enumerate(landings):
        first_hop.append((lvown.at[i], lvin.at[home], row_sem.at[0, n], row_sem.at[1, home], there))
    for n, (i, there) in enumerate(landings):
        first_hop.append((spec_ref.at[:, i], g.at[home, y * 2 + x % 2], own_sem.at[0, n], own_sem.at[1, home], there))
    first_hop = [
        pltpu.make_async_remote_copy(
            src_ref=src, dst_ref=dst, send_sem=ssem, recv_sem=rsem, device_id=there, device_id_type=MESH
        )
        for src, dst, ssem, rsem, there in first_hop
    ]
    for copy in first_hop[:8]:
        copy.start()
    loads[1].wait()
    qcopy = send(qown, qbuf, sib)
    for copy in first_hop[8:]:
        copy.start()

    def landed(ref, sem):
        pltpu.make_async_remote_copy(
            src_ref=ref, dst_ref=ref, send_sem=own_sem.at[0, 0], recv_sem=sem, device_id=sib, device_id_type=MESH
        ).wait_recv()

    for k in range(8):
        landed(lvin.at[k], row_sem.at[1, k])
    part = lvin[0]
    for k in range(1, 8):
        part = part + lvin[k]
    lvall[t] = part
    levels = [send(lvall.at[t], lvall.at[t], t_peer(d)) for d in range(1, 8)]
    qcopy.wait_recv()
    row = pl.ds(2 * z + x % 2, 1)
    use_ref[...] = jnp.where(x // 2 == core, qown[row], qbuf[row]).astype(F32)
    acc[...] = jnp.zeros_like(acc)
    w[NEED] = jnp.zeros_like(w[NEED])
    for copy in levels:
        copy.wait_recv()
    level = lvall[0]
    for n in range(1, 8):
        level = level + lvall[n]
    add_ref[...] = 0.5 * (level / F + 1e-05)
    loads[2].wait()

    def quad(gi, m, q):
        return g.at[gi, m, :, :, pl.ds(pl.multiple_of(q * 256, 256), 256)]

    def hop(gi, m, q, kind, n, there):
        return pltpu.make_async_remote_copy(
            src_ref=quad(gi, m, q),
            dst_ref=quad(gi, m, q),
            send_sem=gsend.at[kind, n, q],
            recv_sem=grecv.at[gi, m, q],
            device_id=there,
            device_id_type=MESH,
        )

    def forward(gi, m, span, kind, n, there):
        def one(q, carry):
            hop(gi, m, q, kind, n, there).start()
            return carry

        lax.fori_loop(span[0], span[1] + 1, one, 0)

    def arrive(gi, m, span):
        def one(q, carry):
            hop(gi, m, q, 0, 0, sib).wait_recv()
            return carry

        lax.fori_loop(span[0], span[1] + 1, one, 0)

    def needs(at):
        return at, jnp.minimum(at + 2, 3)

    def upward(at, relay):
        lone = needs(at)
        return jnp.where(relay, jnp.where(at == 3, 0, at), lone[0]), jnp.where(relay, 3, lone[1])

    def downward(at, relay):
        lone = needs(at)
        return jnp.where(relay, jnp.maximum(at - 1, 0), lone[0]), jnp.where(relay, 3, lone[1])

    above, below, beyond = (y + 1) % 4, (y + 3) % 4, (y + 2) % 4
    mine = needs(y)

    def group_of(n):
        k = n // 2
        zt = jnp.where(k == 0, zs[0], jnp.where(k == 1, zs[1], jnp.where(k == 2, zs[2], zs[3])))
        return zt * 2 + n % 2

    def own(n):
        gi = group_of(n)
        m = y * 2 + par
        landed(g.at[gi, m], own_sem.at[1, gi])
        for c in range(8):
            cols = slice(c * TILE, (c + 1) * TILE)
            re = g[gi, m, 0, :, cols].astype(F32)
            im = g[gi, m, 1, :, cols].astype(F32)
            factor = use_ref[:, cols] / (jnp.sqrt(re * re + im * im) + add_ref[:, cols])
            g[gi, m, 0, :, cols] = (re * factor).astype(BF)
            g[gi, m, 1, :, cols] = (im * factor).astype(BF)
        even = n % 2 == 0
        forward(gi, m, upward(above, even), 0, n, up)
        forward(gi, m, downward(below, jnp.logical_not(even)), 1, n, down)
        forward(gi, m, mine, 2, n, sib)

    def near(n):
        gi = group_of(n)
        even = n % 2 == 0
        m = below * 2 + par
        arrive(gi, m, upward(y, even))

        @pl.when(even)
        def _():
            forward(gi, m, needs(above), 3, n, up)

        forward(gi, m, mine, 4, n, sib)
        m = above * 2 + par
        arrive(gi, m, downward(y, jnp.logical_not(even)))

        @pl.when(jnp.logical_not(even))
        def _():
            forward(gi, m, needs(below), 3, n, down)

        forward(gi, m, mine, 5, n, sib)

    def far(n):
        gi = group_of(n)
        m = beyond * 2 + par
        arrive(gi, m, mine)
        forward(gi, m, mine, 6, n, sib)

    lane = lax.broadcasted_iota(jnp.int32, (FB, TILE), 1)

    def compute(n):
        gi = group_of(n)
        for m in range(4):
            arrive(gi, m * 2 + 1 - par, mine)

        for a in range(NEED):
            cols = tile_at(jnp.minimum(t + a, 7))
            for part in range(2):
                value = g[gi, :, part, :, cols]
                w[a, part] = jnp.where(t + a < 8, value, jnp.zeros_like(value))

        def cross(m, carry):
            rows = pl.ds(pl.multiple_of(m * FB, FB), FB)
            own_re = w[0, 0, m].astype(F32)
            own_im = w[0, 1, m].astype(F32)
            for j in range(NOFF):
                whole = off_ref[j] // 8
                rest = off_ref[j] % 8 * 16
                keep = lane >= rest
                back = (TILE - rest) % TILE
                far_re = jnp.where(keep, w[whole, 0, m].astype(F32), w[whole + 1, 0, m].astype(F32))
                far_im = jnp.where(keep, w[whole, 1, m].astype(F32), w[whole + 1, 1, m].astype(F32))
                far_re = pltpu.roll(far_re, back, 1)
                far_im = pltpu.roll(far_im, back, 1)
                xmat[rows, j * TILE : (j + 1) * TILE] = (own_re * far_re + own_im * far_im).astype(BF)
                xmat[rows, 512 + j * TILE : 512 + (j + 1) * TILE] = (own_im * far_re - own_re * far_im).astype(BF)
            return carry

        lax.fori_loop(0, 8, cross, 0)
        acc[...] += jnp.dot(tab[gi], xmat[...], preferred_element_type=F32)

    def turn(i, carry):
        for stage, first in ((own, 0), (near, 1), (far, 2), (compute, 3)):

            @pl.when((i >= first) & (i < first + 8))
            def _(stage=stage, first=first):
                stage(i - first)

        return carry

    lax.fori_loop(0, 11, turn, 0)

    scale = 1.0 / math.sqrt(F)

    def phases(j):
        left = tile_at(j)
        right = tile_at(j + NOFF)
        a = acc[:HALF, left]
        b = acc[HALF:, right]
        c = acc[HALF:, left]
        d = acc[:HALF, right]
        pos_r = (a - b) * scale
        neg_r = (a + b) * scale
        pos_q = (d + c) * scale
        neg_q = (d - c) * scale
        pos_p = pos_r * pos_r + pos_q * pos_q
        neg_p = neg_r * neg_r + neg_q * neg_q
        mean = jnp.sum(pos_p + neg_p, axis=0, keepdims=True) / LAGS
        floor = 0.25 * (mean + 1e-06)
        pos_d = jnp.sqrt(pos_p + floor)
        neg_d = jnp.sqrt(neg_p + floor)
        p[0, 0, j] = pos_r
        p[1, 0, j] = neg_r
        p[0, 1, j] = pos_r / pos_d
        p[1, 1, j] = neg_r / neg_d
        p[0, 2, j] = pos_q / pos_d
        p[1, 2, j] = neg_q / neg_d

    right, left, across = (x + 1) % 4, (x + 3) % 4, (x + 2) % 4
    phases(across)
    to_right = send(p.at[0, :, across], ring.at[0], x_peer(1))
    to_left = send(p.at[1, :, across], ring.at[1], x_peer(3))
    phases(right)
    plain_right = send(p.at[1, :, right], ringin.at[0], x_peer(1))
    phases(left)
    plain_left = send(p.at[0, :, left], ringin.at[1], x_peer(3))
    phases(x)
    to_right.wait_recv()
    ringsum[0] = ring[0] + p[0, :, right]
    both_right = send(ringsum.at[0], ringin.at[2], x_peer(1))
    to_left.wait_recv()
    ringsum[1] = ring[1] + p[1, :, left]
    both_left = send(ringsum.at[1], ringin.at[3], x_peer(3))
    plain_right.wait_recv()
    plain_left.wait_recv()
    both_right.wait_recv()
    zacc[0] = (p[0, :, x] + ringin[1]) + ringin[2]
    both_left.wait_recv()
    zacc[1] = (p[1, :, x] + ringin[0]) + ringin[3]

    def lag_rows(where):
        return pl.ds(pl.multiple_of(where * 16, 16), 16)

    copies = [
        send(zacc.at[:, :, lag_rows((zall + d) % 8)], zbuf.at[d - 1], z_peer(d)) for d in (4, 3, 5, 2, 6, 1, 7)
    ]
    total = zacc[:, :, lag_rows(zall)]
    for copy in copies:
        copy.wait_recv()
    for d in range(7):
        total = total + zbuf[d]
    linear = total[:, 0] / WINDOWS
    real = total[:, 1] / WINDOWS
    imag = total[:, 2] / WINDOWS
    st[t] = linear * (real * real + imag * imag)

    copies = [send(st.at[t], st.at[t], t_peer(d)) for d in range(1, 8)]
    for copy in copies:
        copy.wait_recv()
    shift = off_ref[x]
    whole = shift // 8
    rest = shift % 8 * 16
    wide = lax.broadcasted_iota(jnp.int32, (2, 16, TILE), 2)
    pieces = []
    for n in range(4):
        tile = 2 * n + y // 2
        first = tile - whole
        a = jnp.where(first >= 0, st[jnp.maximum(first, 0)], 0.0)
        b = jnp.where(first >= 1, st[jnp.maximum(first - 1, 0)], 0.0)
        rev = pltpu.roll(jnp.where(wide < TILE - rest, a, b).reshape(32, TILE), rest, 1).reshape(2, 16, TILE)
        ahead = st[tile]
        pieces.append(ahead[0] + rev[1])
        pieces.append(ahead[1] + rev[0])
    tbuf[...] = jnp.concatenate(pieces, axis=0).T

    def channel_rows(where):
        return pl.ds(pl.multiple_of(y % 2 * 64 + where * 16, 16), 16)

    copies = [send(tbuf.at[channel_rows((x + d) % 4)], jbuf.at[x], x_peer(d)) for d in (1, 2, 3)]
    jbuf[x] = tbuf[channel_rows(x)]
    for copy in copies:
        copy.wait_recv()
    group = lax.broadcasted_iota(jnp.int32, (16, TILE), 1) // 32
    for n in range(4):
        merged = jnp.zeros((16, TILE), F32)
        for j in range(NOFF):
            merged = jnp.where(group == j, pltpu.roll(jbuf[j], (32 * (j - n)) % TILE, 1), merged)
        mbuf[n] = merged
    copies = [send(mbuf.at[(zall + d) % 4], rbuf.at[zall], z_peer(d)) for d in (4, 3, 5, 2, 6, 1, 7)]
    rbuf[zall] = mbuf[zall % 4]
    for copy in copies:
        copy.wait_recv()
    span = lax.broadcasted_iota(jnp.int32, (16, TILE), 1) // 16
    for j in range(NOFF):
        for s in range(2):
            merged = jnp.zeros((16, TILE), F32)
            for n in range(8):
                merged = jnp.where(span == n, pltpu.roll(rbuf[n], (16 * n - 32 * j - 16 * s) % TILE, 1), merged)
            out_ref[j, s] = merged
    for copy in first_hop:
        copy.wait_send()

    def sent(n, carry):
        even = n % 2 == 0
        onward = jnp.where(even, above, below)
        spans = (
            upward(above, even), downward(below, jnp.logical_not(even)), mine, needs(onward), mine, mine, mine,
        )
        for kind, span in enumerate(spans):

            def one(q, inner, kind=kind):
                hop(0, 0, q, kind, n, sib).wait_send()
                return inner

            lax.fori_loop(span[0], span[1] + 1, one, 0)
        return carry

    lax.fori_loop(0, 8, sent, 0)
    for copy in started:
        copy.wait_send()


def whole_window(offsets, spectra, quality, table):
    vmem = pl.BlockSpec(memory_space=pltpu.VMEM)
    return pl.pallas_call(
        window_kernel,
        name="whole_window",
        out_shape=jax.ShapeDtypeStruct((NOFF, 2, 16, TILE), F32),
        in_specs=[pl.BlockSpec(memory_space=pltpu.SMEM)] + [pl.BlockSpec(memory_space=pl.ANY)] * 3,
        out_specs=vmem,
        scratch_shapes=[
            pltpu.VMEM((2, 8, FB, NCH), BF),
            pltpu.VMEM((8, NCH), jnp.int32),
            pltpu.VMEM((8, NCH), jnp.int32),
            pltpu.VMEM((8, 2 * HALF, GROUP), BF),
            pltpu.VMEM((8, 8, 2, FB, NCH), BF),
            pltpu.VMEM((8, 1, NCH), F32),
            pltpu.VMEM((8, 1, NCH), F32),
            pltpu.VMEM((8, 1, NCH), F32),
            pltpu.VMEM((1, NCH), F32),
            pltpu.VMEM((1, NCH), F32),
            pltpu.VMEM((NEED + 1, 2, 8, FB, TILE), BF),
            pltpu.VMEM((GROUP, 2 * NOFF * TILE), BF),
            pltpu.VMEM((2 * HALF, 2 * NOFF * TILE), F32),
            pltpu.VMEM((2, 3, NOFF, HALF, TILE), F32),
            pltpu.VMEM((2, 3, HALF, TILE), F32),
            pltpu.VMEM((2, 3, HALF, TILE), F32),
            pltpu.VMEM((4, 3, HALF, TILE), F32),
            pltpu.VMEM((2, 3, HALF, TILE), F32),
            pltpu.VMEM((7, 2, 3, 16, TILE), F32),
            pltpu.VMEM((8, 2, 16, TILE), F32),
            pltpu.VMEM((TILE, TILE), F32),
            pltpu.VMEM((NOFF, 16, TILE), F32),
            pltpu.VMEM((4, 16, TILE), F32),
            pltpu.VMEM((8, 16, TILE), F32),
            pltpu.SemaphoreType.DMA((3,)),
            pltpu.SemaphoreType.DMA((2, 8)),
            pltpu.SemaphoreType.DMA((2, 8)),
            pltpu.SemaphoreType.DMA((7, 8, 4)),
            pltpu.SemaphoreType.DMA((8, 8, 4)),
            pltpu.SemaphoreType.DMA((40,)),
            pltpu.SemaphoreType.DMA((40,)),
        ],
        compiler_params=pltpu.CompilerParams(collective_id=0, has_side_effects=True),
    )(offsets, spectra, quality, table)


def shards(spectra, quality, offsets):
    table = jnp.asarray(half_table()).astype(BF)
    halves = whole_window(offsets, spectra, quality, table)
    late = jnp.transpose(halves[:, 0], (1, 0, 2))
    early = jnp.flip(jnp.transpose(halves[:, 1], (1, 0, 2)), axis=2)
    return jnp.concatenate([early, late], axis=2)


def solution(mesh):
    return jax.shard_map(
        shards,
        mesh=mesh,
        in_specs=(P(None, "tm", "chan", None), P("tm", None), P()),
        out_specs=P("chan", None, None),
        check_vma=False,
    )
```

```python
import math

import jax
import jax.numpy as jnp
import numpy as np
from jax import lax
from jax.experimental import pallas as pl
from jax.experimental.pallas import tpu as pltpu
from jax.sharding import PartitionSpec as P

MESH = pl.DeviceIdType.MESH
F = 2048
LAGS = 256
HALF = 128
NOFF = 4
WINDOWS = 32
NCH = 1024
TILE = 128
FB = 32
NEED = 5
RAW = 4
GROUP = 256
BF = jnp.bfloat16
F32 = jnp.float32


def place():
    chan = lax.axis_index("chan")
    tm = lax.axis_index("tm")
    return chan // 16, (chan // 4) % 4, chan % 4, tm // 2, tm % 2


def half_table():
    z, half, y, par, low = np.meshgrid(*(np.arange(n) for n in (4, 2, 4, 2, FB)), indexing="ij")
    freq = ((z * 16 + y * 4 + 2 * half + par) * FB + low).reshape(8, 1, GROUP).astype(np.int64)
    lag = (2 * np.arange(HALF, dtype=np.int64) + 1)[None, :, None]
    angle = ((freq * lag) % (4 * F)).astype(np.float64) * (2.0 * math.pi / (4 * F))
    return np.concatenate([np.cos(angle), np.sin(angle)], axis=1).astype(np.float32)


def tile_at(where):
    return pl.ds(pl.multiple_of(where * TILE, TILE), TILE)


def window_kernel(
    off_ref, spec_ref, qual_ref, tab_hbm, out_ref,
    spec, qown, qbuf, tab, g, lvown, lvin, lvall, add_ref, use_ref, w, xmat, acc, p,
    ring, ringsum, ringin, zacc, zbuf, st, tbuf, jbuf, mbuf, rbuf,
    local_sem, own_recv, own_send, row_sem, gsend, grecv, gsib, send_sem, recv_sem,
):
    z, y, x, zh, core = place()
    chan = z * 16 + y * 4 + x
    tm = zh * 2 + core
    sib = (chan, zh * 2 + 1 - core)
    t = y * 2 + core
    zall = zh * 4 + z
    par = (core + x + 1 + x // 2) % 2
    up = (z * 16 + ((y + 1) % 4) * 4 + x, tm)
    down = (z * 16 + ((y + 3) % 4) * 4 + x, tm)

    def x_peer(d):
        return (z * 16 + y * 4 + (x + d) % 4, tm)

    def z_peer(d):
        there = (zall + d) % 8
        return (there % 4 * 16 + y * 4 + x, there // 4 * 2 + core)

    def t_peer(d):
        there = (t + d) % 8
        return (z * 16 + there // 2 * 4 + x, zh * 2 + there % 2)

    mate = z + 1 - 2 * (z % 2)
    zs = [z, mate, 3 - z, 3 - mate]
    spots = [(zs[k], xh) for k in range(4) for xh in (0, 1)]

    loads = [
        pltpu.make_async_copy(src, dst, local_sem.at[n])
        for n, (src, dst) in enumerate(((spec_ref, spec), (qual_ref, qown), (tab_hbm, tab)))
    ]
    for copy in loads:
        copy.start()
    barrier = pltpu.get_barrier_semaphore()
    greet = [(zt * 16 + y * 4 + 2 * xh + par, zh * 2 + x // 2) for zt, xh in spots]
    greet += [x_peer(d) for d in (1, 2, 3)]
    greet += [z_peer(d) for d in range(1, 8)]
    greet += [t_peer(d) for d in range(1, 8)]
    for there in greet:
        pl.semaphore_signal(barrier, inc=1, device_id=there, device_id_type=MESH)
    pl.semaphore_wait(barrier, len(greet))

    def remote(src, dst, ssem, rsem, there):
        return pltpu.make_async_remote_copy(
            src_ref=src, dst_ref=dst, send_sem=ssem, recv_sem=rsem, device_id=there, device_id_type=MESH
        )

    def send(src, dst, out_sem, in_sem, there):
        remote(src, dst, send_sem.at[out_sem], recv_sem.at[in_sem], there).start()

    def received(ref, in_sem):
        remote(ref, ref, send_sem.at[0], recv_sem.at[in_sem], sib).wait_recv()

    def gone(ref, sem):
        remote(ref, ref, sem, recv_sem.at[0], sib).wait_send()

    landings = [
        (2 * zt + low, (zt * 16 + y * 4 + low + 2 * core, zh * 2 + (x + low + 1 + core) % 2)) for zt, low in spots
    ]
    home = z * 2 + x // 2
    first_hop = [
        remote(lvown.at[i], lvin.at[home], row_sem.at[0], row_sem.at[1], there) for i, there in landings
    ]
    for i, there in landings:
        for q in range(4):
            src = spec_ref.at[:, i, :, q * 256 : (q + 1) * 256]
            dst = g.at[home, y * 2 + x % 2, q]
            first_hop.append(remote(src, dst, own_send.at[0], own_recv.at[home, q], there))
    for copy in first_hop[8:24]:
        copy.start()
    loads[0].wait()

    def measure(i, carry):
        re = spec[0, i].astype(F32)
        im = spec[1, i].astype(F32)
        lvown[i] = jnp.sum(jnp.sqrt(re * re + im * im), axis=0, keepdims=True)
        return carry

    lax.fori_loop(0, 8, measure, 0)
    for copy in first_hop[:8]:
        copy.start()
    for copy in first_hop[24:]:
        copy.start()
    loads[1].wait()
    send(qown, qbuf, 0, 0, sib)

    acc[...] = jnp.zeros_like(acc)
    w[NEED] = jnp.zeros_like(w[NEED])

    def hop(gi, m, q, kind, there):
        block = g.at[gi, m, q]
        arrival = gsib.at[gi] if kind == 3 else grecv.at[gi, m // 2, q]
        return remote(block, block, gsend.at[kind], arrival, there)

    def needs(at):
        return at, jnp.minimum(at + 2, 3)

    def upward(at, relay):
        lone = needs(at)
        return jnp.where(relay, jnp.where(at == 3, 0, at), lone[0]), jnp.where(relay, 3, lone[1])

    def downward(at, relay):
        lone = needs(at)
        return jnp.where(relay, jnp.maximum(at - 1, 0), lone[0]), jnp.where(relay, 3, lone[1])

    above, below, beyond = (y + 1) % 4, (y + 3) % 4, (y + 2) % 4
    mine = needs(y)

    def group_of(n):
        k = n // 2
        zt = jnp.where(k == 0, zs[0], jnp.where(k == 1, zs[1], jnp.where(k == 2, zs[2], zs[3])))
        return zt * 2 + n % 2

    def whitened(gi, m, tile):
        cols = tile_at(tile)
        half = tile_at(tile % 2)
        re = g[gi, m, tile // 2, 0, :, half].astype(F32)
        im = g[gi, m, tile // 2, 1, :, half].astype(F32)
        factor = use_ref[:, cols] / (jnp.sqrt(re * re + im * im) + add_ref[:, cols])
        return (re * factor).astype(BF), (im * factor).astype(BF)

    def within(q, span):
        return (q >= span[0]) & (q <= span[1])

    def start_if(wanted, *args):
        @pl.when(wanted)
        def _():
            hop(*args).start()

    def own(n):
        gi = group_of(n)
        m = y * 2 + par
        even = n % 2 == 0

        def one(q, carry):
            block = g.at[gi, m, q]
            remote(block, block, own_send.at[0], own_recv.at[gi, q], sib).wait_recv()

            @pl.when(n >= RAW)
            def _():
                for h in range(2):
                    re, im = whitened(gi, m, q * 2 + h)
                    g[gi, m, q, 0, :, h * TILE : (h + 1) * TILE] = re
                    g[gi, m, q, 1, :, h * TILE : (h + 1) * TILE] = im

            start_if(within(q, upward(above, even)), gi, m, q, 0, up)
            start_if(within(q, downward(below, jnp.logical_not(even))), gi, m, q, 1, down)
            start_if(within(q, mine), gi, m, q, 3, sib)
            return carry

        lax.fori_loop(0, 4, one, 0)

    def relay(gi, m, span, passed, there):
        def one(q, carry):
            hop(gi, m, q, 0, sib).wait_recv()
            start_if(within(q, passed), gi, m, q, 2, there)
            start_if(within(q, mine), gi, m, q, 3, sib)
            return carry

        lax.fori_loop(span[0], span[1] + 1, one, 0)

    def near(n):
        gi = group_of(n)
        even = n % 2 == 0
        lone = needs(above)
        passed = jnp.where(even, lone[0], 4), lone[1]
        relay(gi, below * 2 + par, upward(y, even), passed, up)
        lone = needs(below)
        passed = jnp.where(even, 4, lone[0]), lone[1]
        relay(gi, above * 2 + par, downward(y, jnp.logical_not(even)), passed, down)

    def far(n):
        relay(group_of(n), beyond * 2 + par, mine, (4, 4), up)

    lane = lax.broadcasted_iota(jnp.int32, (FB, TILE), 1)

    def compute(n):
        gi = group_of(n)
        count = mine[1] - mine[0] + 1
        for size in (1, 2, 3):

            @pl.when(count == size)
            def _(size=size):
                block = g.at[gi, pl.ds(0, size)]
                remote(block, block, gsend.at[3], gsib.at[gi], sib).wait_recv()


        @pl.when(n < RAW)
        def _():
            def whiten(m, carry):
                for a in range(NEED):
                    re, im = whitened(gi, m, jnp.minimum(t + a, 7))
                    w[a, 0, m] = jnp.where(t + a < 8, re, jnp.zeros_like(re))
                    w[a, 1, m] = jnp.where(t + a < 8, im, jnp.zeros_like(im))
                return carry

            lax.fori_loop(0, 8, whiten, 0)

        @pl.when(n >= RAW)
        def _():
            for a in range(NEED):
                tile = jnp.minimum(t + a, 7)
                for part in range(2):
                    value = g[gi, :, tile // 2, part, :, tile_at(tile % 2)]
                    w[a, part] = jnp.where(t + a < 8, value, jnp.zeros_like(value))

        def cross(m, carry):
            rows = pl.ds(pl.multiple_of(m * FB, FB), FB)
            own_re = w[0, 0, m].astype(F32)
            own_im = w[0, 1, m].astype(F32)
            for j in range(NOFF):
                whole = off_ref[j] // 8
                rest = off_ref[j] % 8 * 16
                keep = lane >= rest
                back = (TILE - rest) % TILE
                far_re = jnp.where(keep, w[whole, 0, m].astype(F32), w[whole + 1, 0, m].astype(F32))
                far_im = jnp.where(keep, w[whole, 1, m].astype(F32), w[whole + 1, 1, m].astype(F32))
                far_re = pltpu.roll(far_re, back, 1)
                far_im = pltpu.roll(far_im, back, 1)
                xmat[rows, j * TILE : (j + 1) * TILE] = (own_re * far_re + own_im * far_im).astype(BF)
                xmat[rows, 512 + j * TILE : 512 + (j + 1) * TILE] = (own_im * far_re - own_re * far_im).astype(BF)
            return carry

        lax.fori_loop(0, 8, cross, 0)
        acc[...] += jnp.dot(tab[gi], xmat[...], preferred_element_type=F32)

    for n in range(4):
        own(n)
    near(0)
    near(1)
    near(2)
    remote(lvin, lvin, row_sem.at[0], row_sem.at[1], sib).wait_recv()
    part = lvin[0]
    for k in range(1, 8):
        part = part + lvin[k]
    lvall[t] = part
    for d in range(1, 8):
        send(lvall.at[t], lvall.at[t], 1, 1, t_peer(d))
    near(3)
    for n in range(4):
        far(n)
    received(qbuf, 0)
    row = pl.ds(2 * z + x % 2, 1)
    use_ref[...] = jnp.where(x // 2 == core, qown[row], qbuf[row]).astype(F32)
    received(lvall.at[pl.ds(0, 7)], 1)
    level = lvall[0]
    for n in range(1, 8):
        level = level + lvall[n]
    add_ref[...] = 0.5 * (level / F + 1e-05)
    loads[2].wait()

    def turn(i, carry):
        @pl.when(i < 4)
        def _():
            own(i + 4)

        @pl.when((i >= 1) & (i < 5))
        def _():
            near(i + 3)

        @pl.when((i >= 2) & (i < 6))
        def _():
            far(i + 2)

        compute(i)
        return carry

    lax.fori_loop(0, 8, turn, 0)

    scale = 1.0 / math.sqrt(F)

    def phases(j):
        left = tile_at(j)
        right = tile_at(j + NOFF)
        a = acc[:HALF, left]
        b = acc[HALF:, right]
        c = acc[HALF:, left]
        d = acc[:HALF, right]
        pos_r = (a - b) * scale
        neg_r = (a + b) * scale
        pos_q = (d + c) * scale
        neg_q = (d - c) * scale
        pos_p = pos_r * pos_r + pos_q * pos_q
        neg_p = neg_r * neg_r + neg_q * neg_q
        mean = jnp.sum(pos_p + neg_p, axis=0, keepdims=True) / LAGS
        floor = 0.25 * (mean + 1e-06)
        pos_d = jnp.sqrt(pos_p + floor)
        neg_d = jnp.sqrt(neg_p + floor)
        values = ((pos_r, pos_r / pos_d, pos_q / pos_d), (neg_r, neg_r / neg_d, neg_q / neg_d))
        for s in range(2):
            for part in range(3):
                rows = values[s][part].reshape(8, 2, 8, TILE)
                for h in range(2):
                    p[h, s, part, j] = rows[:, h].reshape(64, TILE)

    right, left, across = (x + 1) % 4, (x + 3) % 4, (x + 2) % 4

    def across_out(h):
        send(p.at[h, 0, :, across], ring.at[h, 0], 2, 2 + 6 * h, x_peer(1))
        send(p.at[h, 1, :, across], ring.at[h, 1], 2, 3 + 6 * h, x_peer(3))

    def plain_out(h):
        send(p.at[h, 1, :, right], ringin.at[h, 0], 3, 4 + 6 * h, x_peer(1))
        send(p.at[h, 0, :, left], ringin.at[h, 1], 3, 5 + 6 * h, x_peer(3))

    def both_out(h):
        received(ring.at[h, 0], 2 + 6 * h)
        ringsum[h, 0] = ring[h, 0] + p[h, 0, :, right]
        send(ringsum.at[h, 0], ringin.at[h, 2], 3, 6 + 6 * h, x_peer(1))
        received(ring.at[h, 1], 3 + 6 * h)
        ringsum[h, 1] = ring[h, 1] + p[h, 1, :, left]
        send(ringsum.at[h, 1], ringin.at[h, 3], 3, 7 + 6 * h, x_peer(3))

    def lag_rows(where):
        return pl.ds(pl.multiple_of(where * 8, 8), 8)

    def z_out(h):
        for n in range(4):
            received(ringin.at[h, n], 4 + 6 * h + n)
        zacc[h, 0] = (p[h, 0, :, x] + ringin[h, 1]) + ringin[h, 2]
        zacc[h, 1] = (p[h, 1, :, x] + ringin[h, 0]) + ringin[h, 3]
        for d in (4, 3, 5, 2, 6, 1, 7):
            send(zacc.at[h, :, :, lag_rows((zall + d) % 8)], zbuf.at[h, d - 1], 4 + h, 14 + h, z_peer(d))

    def z_in(h):
        received(zbuf.at[h], 14 + h)
        total = zacc[h, :, :, lag_rows(zall)]
        for d in range(7):
            total = total + zbuf[h, d]
        linear = total[:, 0] / WINDOWS
        real = total[:, 1] / WINDOWS
        imag = total[:, 2] / WINDOWS
        st[t, :, 8 * h : 8 * h + 8] = linear * (real * real + imag * imag)

    phases(across)
    across_out(0)
    phases(right)
    phases(left)
    plain_out(0)
    across_out(1)
    phases(x)
    both_out(0)
    plain_out(1)
    both_out(1)
    z_out(0)
    z_out(1)
    z_in(0)
    z_in(1)

    for d in range(1, 8):
        send(st.at[t], st.at[t], 6, 16, t_peer(d))
    received(st.at[pl.ds(0, 7)], 16)
    shift = off_ref[x]
    whole = shift // 8
    rest = shift % 8 * 16
    wide = lax.broadcasted_iota(jnp.int32, (2, 16, TILE), 2)
    pieces = []
    for n in range(4):
        tile = 2 * n + y // 2
        first = tile - whole
        a = jnp.where(first >= 0, st[jnp.maximum(first, 0)], 0.0)
        b = jnp.where(first >= 1, st[jnp.maximum(first - 1, 0)], 0.0)
        rev = pltpu.roll(jnp.where(wide < TILE - rest, a, b).reshape(32, TILE), rest, 1).reshape(2, 16, TILE)
        ahead = st[tile]
        pieces.append(ahead[0] + rev[1])
        pieces.append(ahead[1] + rev[0])
    tbuf[...] = jnp.concatenate(pieces, axis=0).T

    def channel_rows(where):
        return pl.ds(pl.multiple_of(y % 2 * 64 + where * 16, 16), 16)

    for d in (1, 2, 3):
        send(tbuf.at[channel_rows((x + d) % 4)], jbuf.at[x], 7, 17, x_peer(d))
    jbuf[x] = tbuf[channel_rows(x)]
    received(jbuf.at[pl.ds(0, 3)], 17)
    group = lax.broadcasted_iota(jnp.int32, (16, TILE), 1) // 32
    for n in range(4):
        merged = jnp.zeros((16, TILE), F32)
        for j in range(NOFF):
            merged = jnp.where(group == j, pltpu.roll(jbuf[j], (32 * (j - n)) % TILE, 1), merged)
        mbuf[n] = merged
    for d in (4, 3, 5, 2, 6, 1, 7):
        send(mbuf.at[(zall + d) % 4], rbuf.at[zall], 8, 18, z_peer(d))
    rbuf[zall] = mbuf[zall % 4]
    received(rbuf.at[pl.ds(0, 7)], 18)
    spot = lax.broadcasted_iota(jnp.int32, (16, TILE), 1)
    span = spot // 16
    for j in range(NOFF):
        for s in range(2):
            merged = jnp.zeros((16, TILE), F32)
            for n in range(8):
                at = 7 - n if s else n
                merged = jnp.where(span == at, pltpu.roll(rbuf[n], (16 * at - 32 * j - 16 * s) % TILE, 1), merged)
            if s:
                for bit in (1, 2, 4, 8):
                    merged = jnp.where(
                        spot // bit % 2 == 1, pltpu.roll(merged, bit, 1), pltpu.roll(merged, TILE - bit, 1)
                    )
            out_ref[:, j, (1 - s) * HALF : (2 - s) * HALF] = merged

    gone(lvown, row_sem.at[0])
    gone(g.at[0], own_send.at[0])
    gone(qown, send_sem.at[0])
    gone(lvall.at[pl.ds(0, 7)], send_sem.at[1])
    gone(ring, send_sem.at[2])
    gone(ringin, send_sem.at[3])
    for h in range(2):
        gone(zbuf.at[h], send_sem.at[4 + h])
    gone(st.at[pl.ds(0, 7)], send_sem.at[6])
    gone(jbuf.at[pl.ds(0, 3)], send_sem.at[7])
    gone(rbuf.at[pl.ds(0, 7)], send_sem.at[8])
    width = (3, 3, 2, 1)
    for at in range(4):
        ahead, behind = (at + 1) % 4, (at + 3) % 4
        upper = (4, 3, 2, 4)[ahead]
        lower = (4, 4, 3, 2)[behind]

        @pl.when(y == at)
        def _(at=at, ahead=ahead, behind=behind, upper=upper, lower=lower):
            gone(g.at[0, pl.ds(0, upper + width[ahead])], gsend.at[0])
            gone(g.at[0, pl.ds(0, lower + width[behind])], gsend.at[1])
            gone(g.at[0, pl.ds(0, width[ahead] + width[behind])], gsend.at[2])
            gone(g.at[pl.ds(0, width[at])], gsend.at[3])


def whole_window(offsets, spectra, quality, table):
    vmem = pl.BlockSpec(memory_space=pltpu.VMEM)
    return pl.pallas_call(
        window_kernel,
        name="whole_window",
        out_shape=jax.ShapeDtypeStruct((16, NOFF, LAGS), F32),
        in_specs=[pl.BlockSpec(memory_space=pltpu.SMEM)] + [pl.BlockSpec(memory_space=pl.ANY)] * 3,
        out_specs=vmem,
        scratch_shapes=[
            pltpu.VMEM((2, 8, FB, NCH), BF),
            pltpu.VMEM((8, NCH), jnp.int32),
            pltpu.VMEM((8, NCH), jnp.int32),
            pltpu.VMEM((8, 2 * HALF, GROUP), BF),
            pltpu.VMEM((8, 8, 4, 2, FB, 256), BF),
            pltpu.VMEM((8, 1, NCH), F32),
            pltpu.VMEM((8, 1, NCH), F32),
            pltpu.VMEM((8, 1, NCH), F32),
            pltpu.VMEM((1, NCH), F32),
            pltpu.VMEM((1, NCH), F32),
            pltpu.VMEM((NEED + 1, 2, 8, FB, TILE), BF),
            pltpu.VMEM((GROUP, 2 * NOFF * TILE), BF),
            pltpu.VMEM((2 * HALF, 2 * NOFF * TILE), F32),
            pltpu.VMEM((2, 2, 3, NOFF, 64, TILE), F32),
            pltpu.VMEM((2, 2, 3, 64, TILE), F32),
            pltpu.VMEM((2, 2, 3, 64, TILE), F32),
            pltpu.VMEM((2, 4, 3, 64, TILE), F32),
            pltpu.VMEM((2, 2, 3, 64, TILE), F32),
            pltpu.VMEM((2, 7, 2, 3, 8, TILE), F32),
            pltpu.VMEM((8, 2, 16, TILE), F32),
            pltpu.VMEM((TILE, TILE), F32),
            pltpu.VMEM((NOFF, 16, TILE), F32),
            pltpu.VMEM((4, 16, TILE), F32),
            pltpu.VMEM((8, 16, TILE), F32),
            pltpu.SemaphoreType.DMA((3,)),
            pltpu.SemaphoreType.DMA((8, 4)),
            pltpu.SemaphoreType.DMA((1,)),
            pltpu.SemaphoreType.DMA((2,)),
            pltpu.SemaphoreType.DMA((4,)),
            pltpu.SemaphoreType.DMA((8, 4, 4)),
            pltpu.SemaphoreType.DMA((8,)),
            pltpu.SemaphoreType.DMA((9,)),
            pltpu.SemaphoreType.DMA((19,)),
        ],
        compiler_params=pltpu.CompilerParams(collective_id=0, has_side_effects=True),
    )(offsets, spectra, quality, table)


def shards(spectra, quality, offsets):
    table = jnp.asarray(half_table()).astype(BF)
    return whole_window(offsets, spectra, quality, table)


def solution(mesh):
    return jax.shard_map(
        shards,
        mesh=mesh,
        in_specs=(P(None, "tm", "chan", None), P("tm", None), P()),
        out_specs=P("chan", None, None),
        check_vma=False,
    )
```

```python
import math

import jax
import jax.numpy as jnp
import numpy as np
from jax import lax
from jax.experimental import pallas as pl
from jax.experimental.pallas import tpu as pltpu
from jax.sharding import PartitionSpec as P

MESH = pl.DeviceIdType.MESH
F = 2048
LAGS = 256
HALF = 128
NOFF = 4
WINDOWS = 32
NCH = 1024
TILE = 128
FB = 32
NEED = 5
RAW = 4
GROUP = 256
BF = jnp.bfloat16
F32 = jnp.float32


def place():
    chan = lax.axis_index("chan")
    tm = lax.axis_index("tm")
    return chan // 16, (chan // 4) % 4, chan % 4, tm // 2, tm % 2


def half_table():
    z, half, y, par, low = np.meshgrid(*(np.arange(n) for n in (4, 2, 4, 2, FB)), indexing="ij")
    freq = ((z * 16 + y * 4 + 2 * half + par) * FB + low).reshape(8, 1, GROUP).astype(np.int64)
    lag = (2 * np.arange(HALF, dtype=np.int64) + 1)[None, :, None]
    angle = ((freq * lag) % (4 * F)).astype(np.float64) * (2.0 * math.pi / (4 * F))
    return np.concatenate([np.cos(angle), np.sin(angle)], axis=1).astype(np.float32)


def tile_at(where):
    return pl.ds(pl.multiple_of(where * TILE, TILE), TILE)


def window_kernel(
    off_ref, spec_ref, qual_ref, tab_hbm, out_ref,
    spec, qown, qbuf, tab, g, lvown, lvin, lvall, add_ref, use_ref, w, xmat, acc, p,
    ring, ringsum, ringin, zacc, zbuf, st, tbuf, jbuf, mbuf, rbuf,
    local_sem, own_recv, own_send, row_sem, gsend, grecv, gsib, send_sem, recv_sem,
):
    z, y, x, zh, core = place()
    chan = z * 16 + y * 4 + x
    tm = zh * 2 + core
    sib = (chan, zh * 2 + 1 - core)
    t = y * 2 + core
    zall = zh * 4 + z
    par = (core + x + 1 + x // 2) % 2
    up = (z * 16 + ((y + 1) % 4) * 4 + x, tm)
    down = (z * 16 + ((y + 3) % 4) * 4 + x, tm)

    def x_peer(d):
        return (z * 16 + y * 4 + (x + d) % 4, tm)

    def z_peer(d):
        there = (zall + d) % 8
        return (there % 4 * 16 + y * 4 + x, there // 4 * 2 + core)

    def t_peer(d):
        there = (t + d) % 8
        return (z * 16 + there // 2 * 4 + x, zh * 2 + there % 2)

    mate = z + 1 - 2 * (z % 2)
    zs = [z, mate, 3 - z, 3 - mate]
    spots = [(zs[k], xh) for k in range(4) for xh in (0, 1)]

    loads = [
        pltpu.make_async_copy(src, dst, local_sem.at[n])
        for n, (src, dst) in enumerate(((spec_ref, spec), (qual_ref, qown), (tab_hbm, tab)))
    ]
    for copy in loads:
        copy.start()
    barrier = pltpu.get_barrier_semaphore()
    greet = [(zt * 16 + y * 4 + 2 * xh + par, zh * 2 + x // 2) for zt, xh in spots]
    greet += [x_peer(d) for d in (1, 2, 3)]
    greet += [z_peer(d) for d in range(1, 8)]
    greet += [t_peer(d) for d in range(1, 8)]
    for there in greet:
        pl.semaphore_signal(barrier, inc=1, device_id=there, device_id_type=MESH)
    pl.semaphore_wait(barrier, len(greet))

    def remote(src, dst, ssem, rsem, there):
        return pltpu.make_async_remote_copy(
            src_ref=src, dst_ref=dst, send_sem=ssem, recv_sem=rsem, device_id=there, device_id_type=MESH
        )

    def send(src, dst, out_sem, in_sem, there):
        remote(src, dst, send_sem.at[out_sem], recv_sem.at[in_sem], there).start()

    def received(ref, in_sem):
        remote(ref, ref, send_sem.at[0], recv_sem.at[in_sem], sib).wait_recv()

    def gone(ref, sem):
        remote(ref, ref, sem, recv_sem.at[0], sib).wait_send()

    landings = [
        (2 * zt + low, (zt * 16 + y * 4 + low + 2 * core, zh * 2 + (x + low + 1 + core) % 2)) for zt, low in spots
    ]
    home = z * 2 + x // 2
    first_hop = [
        remote(lvown.at[i], lvin.at[home], row_sem.at[0], row_sem.at[1], there) for i, there in landings
    ]
    for i, there in landings:
        for q in range(4):
            src = spec_ref.at[:, i, :, q * 256 : (q + 1) * 256]
            dst = g.at[home, y * 2 + x % 2, q]
            first_hop.append(remote(src, dst, own_send.at[0], own_recv.at[home, q], there))
    for copy in first_hop[8:24]:
        copy.start()
    loads[0].wait()

    def measure(i, carry):
        re = spec[0, i].astype(F32)
        im = spec[1, i].astype(F32)
        lvown[i] = jnp.sum(jnp.sqrt(re * re + im * im), axis=0, keepdims=True)
        return carry

    lax.fori_loop(0, 8, measure, 0)
    for copy in first_hop[:8]:
        copy.start()
    for copy in first_hop[24:]:
        copy.start()
    loads[1].wait()
    send(qown, qbuf, 0, 0, sib)

    acc[...] = jnp.zeros_like(acc)
    w[NEED] = jnp.zeros_like(w[NEED])

    def hop(gi, m, q, kind, there):
        block = g.at[gi, m, q]
        arrival = gsib.at[gi] if kind == 3 else grecv.at[gi, m // 2, q]
        return remote(block, block, gsend.at[kind], arrival, there)

    def needs(at):
        return at, jnp.minimum(at + 2, 3)

    def upward(at, relay):
        lone = needs(at)
        return jnp.where(relay, jnp.where(at == 3, 0, at), lone[0]), jnp.where(relay, 3, lone[1])

    def downward(at, relay):
        lone = needs(at)
        return jnp.where(relay, jnp.maximum(at - 1, 0), lone[0]), jnp.where(relay, 3, lone[1])

    above, below, beyond = (y + 1) % 4, (y + 3) % 4, (y + 2) % 4
    mine = needs(y)

    def group_of(n):
        k = n // 2
        zt = jnp.where(k == 0, zs[0], jnp.where(k == 1, zs[1], jnp.where(k == 2, zs[2], zs[3])))
        return zt * 2 + n % 2

    def whitened(gi, m, tile):
        cols = tile_at(tile)
        half = tile_at(tile % 2)
        re = g[gi, m, tile // 2, 0, :, half].astype(F32)
        im = g[gi, m, tile // 2, 1, :, half].astype(F32)
        factor = use_ref[:, cols] / (jnp.sqrt(re * re + im * im) + add_ref[:, cols])
        return (re * factor).astype(BF), (im * factor).astype(BF)

    def within(q, span):
        return (q >= span[0]) & (q <= span[1])

    def start_if(wanted, *args):
        @pl.when(wanted)
        def _():
            hop(*args).start()

    def own(n):
        gi = group_of(n)
        m = y * 2 + par
        even = n % 2 == 0

        def one(q, carry):
            block = g.at[gi, m, q]
            remote(block, block, own_send.at[0], own_recv.at[gi, q], sib).wait_recv()

            @pl.when(n >= RAW)
            def _():
                for h in range(2):
                    re, im = whitened(gi, m, q * 2 + h)
                    g[gi, m, q, 0, :, h * TILE : (h + 1) * TILE] = re
                    g[gi, m, q, 1, :, h * TILE : (h + 1) * TILE] = im

            start_if(within(q, upward(above, even)), gi, m, q, 0, up)
            start_if(within(q, downward(below, jnp.logical_not(even))), gi, m, q, 1, down)
            start_if(within(q, mine), gi, m, q, 3, sib)
            return carry

        lax.fori_loop(0, 4, one, 0)

    def relay(gi, m, span, passed, there):
        def one(q, carry):
            hop(gi, m, q, 0, sib).wait_recv()
            start_if(within(q, passed), gi, m, q, 2, there)
            start_if(within(q, mine), gi, m, q, 3, sib)
            return carry

        lax.fori_loop(span[0], span[1] + 1, one, 0)

    def near(n):
        gi = group_of(n)
        even = n % 2 == 0
        lone = needs(above)
        passed = jnp.where(even, lone[0], 4), lone[1]
        relay(gi, below * 2 + par, upward(y, even), passed, up)
        lone = needs(below)
        passed = jnp.where(even, 4, lone[0]), lone[1]
        relay(gi, above * 2 + par, downward(y, jnp.logical_not(even)), passed, down)

    def far(n):
        relay(group_of(n), beyond * 2 + par, mine, (4, 4), up)

    lane = lax.broadcasted_iota(jnp.int32, (FB, TILE), 1)

    def compute(n):
        gi = group_of(n)
        count = mine[1] - mine[0] + 1
        for size in (1, 2, 3):

            @pl.when(count == size)
            def _(size=size):
                block = g.at[gi, pl.ds(0, size)]
                remote(block, block, gsend.at[3], gsib.at[gi], sib).wait_recv()


        @pl.when(n < RAW)
        def _():
            def whiten(m, carry):
                for a in range(NEED):
                    re, im = whitened(gi, m, jnp.minimum(t + a, 7))
                    w[a, 0, m] = jnp.where(t + a < 8, re, jnp.zeros_like(re))
                    w[a, 1, m] = jnp.where(t + a < 8, im, jnp.zeros_like(im))
                return carry

            lax.fori_loop(0, 8, whiten, 0, unroll=4)

        @pl.when(n >= RAW)
        def _():
            for a in range(NEED):
                tile = jnp.minimum(t + a, 7)
                for part in range(2):
                    value = g[gi, :, tile // 2, part, :, tile_at(tile % 2)]
                    w[a, part] = jnp.where(t + a < 8, value, jnp.zeros_like(value))

        def cross(m, carry):
            rows = pl.ds(pl.multiple_of(m * FB, FB), FB)
            own_re = w[0, 0, m].astype(F32)
            own_im = w[0, 1, m].astype(F32)
            for j in range(NOFF):
                whole = off_ref[j] // 8
                rest = off_ref[j] % 8 * 16
                keep = lane >= rest
                back = (TILE - rest) % TILE
                far_re = jnp.where(keep, w[whole, 0, m].astype(F32), w[whole + 1, 0, m].astype(F32))
                far_im = jnp.where(keep, w[whole, 1, m].astype(F32), w[whole + 1, 1, m].astype(F32))
                far_re = pltpu.roll(far_re, back, 1)
                far_im = pltpu.roll(far_im, back, 1)
                xmat[rows, j * TILE : (j + 1) * TILE] = (own_re * far_re + own_im * far_im).astype(BF)
                xmat[rows, 512 + j * TILE : 512 + (j + 1) * TILE] = (own_im * far_re - own_re * far_im).astype(BF)
            return carry

        lax.fori_loop(0, 8, cross, 0, unroll=8)
        acc[...] += jnp.dot(tab[gi], xmat[...], preferred_element_type=F32)

    for n in range(4):
        own(n)
    near(0)
    near(1)
    near(2)
    remote(lvin, lvin, row_sem.at[0], row_sem.at[1], sib).wait_recv()
    part = lvin[0]
    for k in range(1, 8):
        part = part + lvin[k]
    lvall[t] = part
    for d in range(1, 8):
        send(lvall.at[t], lvall.at[t], 1, 1, t_peer(d))
    near(3)
    for n in range(4):
        far(n)
    received(qbuf, 0)
    row = pl.ds(2 * z + x % 2, 1)
    use_ref[...] = jnp.where(x // 2 == core, qown[row], qbuf[row]).astype(F32)
    received(lvall.at[pl.ds(0, 7)], 1)
    level = lvall[0]
    for n in range(1, 8):
        level = level + lvall[n]
    add_ref[...] = 0.5 * (level / F + 1e-05)
    loads[2].wait()

    def turn(i, carry):
        @pl.when(i < 4)
        def _():
            own(i + 4)

        @pl.when((i >= 1) & (i < 5))
        def _():
            near(i + 3)

        @pl.when((i >= 2) & (i < 6))
        def _():
            far(i + 2)

        compute(i)
        return carry

    lax.fori_loop(0, 8, turn, 0)

    scale = 1.0 / math.sqrt(F)

    def phases(j):
        left = tile_at(j)
        right = tile_at(j + NOFF)
        a = acc[:HALF, left]
        b = acc[HALF:, right]
        c = acc[HALF:, left]
        d = acc[:HALF, right]
        pos_r = (a - b) * scale
        neg_r = (a + b) * scale
        pos_q = (d + c) * scale
        neg_q = (d - c) * scale
        pos_p = pos_r * pos_r + pos_q * pos_q
        neg_p = neg_r * neg_r + neg_q * neg_q
        mean = jnp.sum(pos_p + neg_p, axis=0, keepdims=True) / LAGS
        floor = 0.25 * (mean + 1e-06)
        pos_d = jnp.sqrt(pos_p + floor)
        neg_d = jnp.sqrt(neg_p + floor)
        values = ((pos_r, pos_r / pos_d, pos_q / pos_d), (neg_r, neg_r / neg_d, neg_q / neg_d))
        for s in range(2):
            for part in range(3):
                rows = values[s][part].reshape(8, 2, 8, TILE)
                for h in range(2):
                    p[h, s, part, j] = rows[:, h].reshape(64, TILE)

    right, left, across = (x + 1) % 4, (x + 3) % 4, (x + 2) % 4

    def across_out(h):
        send(p.at[h, 0, :, across], ring.at[h, 0], 2, 2 + 6 * h, x_peer(1))
        send(p.at[h, 1, :, across], ring.at[h, 1], 2, 3 + 6 * h, x_peer(3))

    def plain_out(h):
        send(p.at[h, 1, :, right], ringin.at[h, 0], 3, 4 + 6 * h, x_peer(1))
        send(p.at[h, 0, :, left], ringin.at[h, 1], 3, 5 + 6 * h, x_peer(3))

    def both_out(h):
        received(ring.at[h, 0], 2 + 6 * h)
        ringsum[h, 0] = ring[h, 0] + p[h, 0, :, right]
        send(ringsum.at[h, 0], ringin.at[h, 2], 3, 6 + 6 * h, x_peer(1))
        received(ring.at[h, 1], 3 + 6 * h)
        ringsum[h, 1] = ring[h, 1] + p[h, 1, :, left]
        send(ringsum.at[h, 1], ringin.at[h, 3], 3, 7 + 6 * h, x_peer(3))

    def lag_rows(where):
        return pl.ds(pl.multiple_of(where * 8, 8), 8)

    def z_out(h):
        for n in range(4):
            received(ringin.at[h, n], 4 + 6 * h + n)
        zacc[h, 0] = (p[h, 0, :, x] + ringin[h, 1]) + ringin[h, 2]
        zacc[h, 1] = (p[h, 1, :, x] + ringin[h, 0]) + ringin[h, 3]
        for d in (4, 3, 5, 2, 6, 1, 7):
            send(zacc.at[h, :, :, lag_rows((zall + d) % 8)], zbuf.at[h, d - 1], 4 + h, 14 + h, z_peer(d))

    def z_in(h):
        received(zbuf.at[h], 14 + h)
        total = zacc[h, :, :, lag_rows(zall)]
        for d in range(7):
            total = total + zbuf[h, d]
        linear = total[:, 0] / WINDOWS
        real = total[:, 1] / WINDOWS
        imag = total[:, 2] / WINDOWS
        st[h, t] = linear * (real * real + imag * imag)
        for d in range(1, 8):
            send(st.at[h, t], st.at[h, t], 6, 16 + h, t_peer(d))

    phases(across)
    across_out(0)
    phases(right)
    phases(left)
    plain_out(0)
    across_out(1)
    phases(x)
    both_out(0)
    plain_out(1)
    both_out(1)
    z_out(0)
    z_out(1)
    z_in(0)
    z_in(1)

    for h in range(2):
        received(st.at[h, pl.ds(0, 7)], 16 + h)
    shift = off_ref[x]
    whole = shift // 8
    rest = shift % 8 * 16
    wide = lax.broadcasted_iota(jnp.int32, (32, TILE), 1)

    def stack(tile):
        return jnp.concatenate([st[h, tile, s] for s in range(2) for h in range(2)], axis=0)

    pieces = []
    for n in range(4):
        tile = 2 * n + y // 2
        first = tile - whole
        a = jnp.where(first >= 0, stack(jnp.maximum(first, 0)), 0.0)
        b = jnp.where(first >= 1, stack(jnp.maximum(first - 1, 0)), 0.0)
        rev = pltpu.roll(jnp.where(wide < TILE - rest, a, b), rest, 1)
        ahead = stack(tile)
        pieces.append(ahead[:16] + rev[16:])
        pieces.append(ahead[16:] + rev[:16])
    tbuf[...] = jnp.concatenate(pieces, axis=0).T

    def channel_rows(where):
        return pl.ds(pl.multiple_of(y % 2 * 64 + where * 16, 16), 16)

    for d in (1, 2, 3):
        send(tbuf.at[channel_rows((x + d) % 4)], jbuf.at[x], 7, 18, x_peer(d))
    jbuf[x] = tbuf[channel_rows(x)]
    received(jbuf.at[pl.ds(0, 3)], 18)
    group = lax.broadcasted_iota(jnp.int32, (16, TILE), 1) // 32
    for n in range(4):
        merged = jnp.zeros((16, TILE), F32)
        for j in range(NOFF):
            merged = jnp.where(group == j, pltpu.roll(jbuf[j], (32 * (j - n)) % TILE, 1), merged)
        mbuf[n] = merged
    for d in (4, 3, 5, 2, 6, 1, 7):
        send(mbuf.at[(zall + d) % 4], rbuf.at[zall], 8, 19, z_peer(d))
    rbuf[zall] = mbuf[zall % 4]
    received(rbuf.at[pl.ds(0, 7)], 19)
    spot = lax.broadcasted_iota(jnp.int32, (16, TILE), 1)
    span = spot // 16
    for j in range(NOFF):
        for s in range(2):
            merged = jnp.zeros((16, TILE), F32)
            for n in range(8):
                at = 7 - n if s else n
                merged = jnp.where(span == at, pltpu.roll(rbuf[n], (16 * at - 32 * j - 16 * s) % TILE, 1), merged)
            if s:
                for bit in (1, 2, 4, 8):
                    merged = jnp.where(
                        spot // bit % 2 == 1, pltpu.roll(merged, bit, 1), pltpu.roll(merged, TILE - bit, 1)
                    )
            out_ref[:, j, (1 - s) * HALF : (2 - s) * HALF] = merged

    gone(lvown, row_sem.at[0])
    gone(g.at[0], own_send.at[0])
    gone(qown, send_sem.at[0])
    gone(lvall.at[pl.ds(0, 7)], send_sem.at[1])
    gone(ring, send_sem.at[2])
    gone(ringin, send_sem.at[3])
    for h in range(2):
        gone(zbuf.at[h], send_sem.at[4 + h])
    gone(st.at[:, pl.ds(0, 7)], send_sem.at[6])
    gone(jbuf.at[pl.ds(0, 3)], send_sem.at[7])
    gone(rbuf.at[pl.ds(0, 7)], send_sem.at[8])
    width = (3, 3, 2, 1)
    for at in range(4):
        ahead, behind = (at + 1) % 4, (at + 3) % 4
        upper = (4, 3, 2, 4)[ahead]
        lower = (4, 4, 3, 2)[behind]

        @pl.when(y == at)
        def _(at=at, ahead=ahead, behind=behind, upper=upper, lower=lower):
            gone(g.at[0, pl.ds(0, upper + width[ahead])], gsend.at[0])
            gone(g.at[0, pl.ds(0, lower + width[behind])], gsend.at[1])
            gone(g.at[0, pl.ds(0, width[ahead] + width[behind])], gsend.at[2])
            gone(g.at[pl.ds(0, width[at])], gsend.at[3])


def whole_window(offsets, spectra, quality, table):
    vmem = pl.BlockSpec(memory_space=pltpu.VMEM)
    return pl.pallas_call(
        window_kernel,
        name="whole_window",
        out_shape=jax.ShapeDtypeStruct((16, NOFF, LAGS), F32),
        in_specs=[pl.BlockSpec(memory_space=pltpu.SMEM)] + [pl.BlockSpec(memory_space=pl.ANY)] * 3,
        out_specs=vmem,
        scratch_shapes=[
            pltpu.VMEM((2, 8, FB, NCH), BF),
            pltpu.VMEM((8, NCH), jnp.int32),
            pltpu.VMEM((8, NCH), jnp.int32),
            pltpu.VMEM((8, 2 * HALF, GROUP), BF),
            pltpu.VMEM((8, 8, 4, 2, FB, 256), BF),
            pltpu.VMEM((8, 1, NCH), F32),
            pltpu.VMEM((8, 1, NCH), F32),
            pltpu.VMEM((8, 1, NCH), F32),
            pltpu.VMEM((1, NCH), F32),
            pltpu.VMEM((1, NCH), F32),
            pltpu.VMEM((NEED + 1, 2, 8, FB, TILE), BF),
            pltpu.VMEM((GROUP, 2 * NOFF * TILE), BF),
            pltpu.VMEM((2 * HALF, 2 * NOFF * TILE), F32),
            pltpu.VMEM((2, 2, 3, NOFF, 64, TILE), F32),
            pltpu.VMEM((2, 2, 3, 64, TILE), F32),
            pltpu.VMEM((2, 2, 3, 64, TILE), F32),
            pltpu.VMEM((2, 4, 3, 64, TILE), F32),
            pltpu.VMEM((2, 2, 3, 64, TILE), F32),
            pltpu.VMEM((2, 7, 2, 3, 8, TILE), F32),
            pltpu.VMEM((2, 8, 2, 8, TILE), F32),
            pltpu.VMEM((TILE, TILE), F32),
            pltpu.VMEM((NOFF, 16, TILE), F32),
            pltpu.VMEM((4, 16, TILE), F32),
            pltpu.VMEM((8, 16, TILE), F32),
            pltpu.SemaphoreType.DMA((3,)),
            pltpu.SemaphoreType.DMA((8, 4)),
            pltpu.SemaphoreType.DMA((1,)),
            pltpu.SemaphoreType.DMA((2,)),
            pltpu.SemaphoreType.DMA((4,)),
            pltpu.SemaphoreType.DMA((8, 4, 4)),
            pltpu.SemaphoreType.DMA((8,)),
            pltpu.SemaphoreType.DMA((9,)),
            pltpu.SemaphoreType.DMA((20,)),
        ],
        compiler_params=pltpu.CompilerParams(collective_id=0, has_side_effects=True),
    )(offsets, spectra, quality, table)


def shards(spectra, quality, offsets):
    table = jnp.asarray(half_table()).astype(BF)
    return whole_window(offsets, spectra, quality, table)


def solution(mesh):
    return jax.shard_map(
        shards,
        mesh=mesh,
        in_specs=(P(None, "tm", "chan", None), P("tm", None), P()),
        out_specs=P("chan", None, None),
        check_vma=False,
    )
```

```python
import math

import jax
import jax.numpy as jnp
import numpy as np
from jax import lax
from jax.experimental import pallas as pl
from jax.experimental.pallas import tpu as pltpu
from jax.sharding import PartitionSpec as P

MESH = pl.DeviceIdType.MESH
F = 2048
LAGS = 256
HALF = 128
NOFF = 4
WINDOWS = 32
NCH = 1024
TILE = 128
FB = 32
NEED = 5
RAW = 4
GROUP = 256
BF = jnp.bfloat16
F32 = jnp.float32


def place():
    chan = lax.axis_index("chan")
    tm = lax.axis_index("tm")
    return chan // 16, (chan // 4) % 4, chan % 4, tm // 2, tm % 2


def half_table():
    z, half, y, par, low = np.meshgrid(*(np.arange(n) for n in (4, 2, 4, 2, FB)), indexing="ij")
    freq = ((z * 16 + y * 4 + 2 * half + par) * FB + low).reshape(8, 1, GROUP).astype(np.int64)
    lag = (2 * np.arange(HALF, dtype=np.int64) + 1)[None, :, None]
    angle = ((freq * lag) % (4 * F)).astype(np.float64) * (2.0 * math.pi / (4 * F))
    return np.concatenate([np.cos(angle), np.sin(angle)], axis=1).astype(np.float32)


def tile_at(where):
    return pl.ds(pl.multiple_of(where * TILE, TILE), TILE)


def window_kernel(
    off_ref, spec_ref, qual_ref, tab_hbm, out_ref,
    spec, qown, qbuf, tab, g, lvown, lvin, lvall, add_ref, use_ref, w, xmat, acc, p,
    pair, ring, ringsum, ringin, zacc, zbuf, st, tbuf, jbuf, mbuf, rbuf,
    local_sem, own_recv, own_send, row_sem, gsend, grecv, gsib, send_sem, recv_sem,
):
    z, y, x, zh, core = place()
    chan = z * 16 + y * 4 + x
    tm = zh * 2 + core
    sib = (chan, zh * 2 + 1 - core)
    t = y * 2 + core
    zall = zh * 4 + z
    par = (core + x + 1 + x // 2) % 2
    up = (z * 16 + ((y + 1) % 4) * 4 + x, tm)
    down = (z * 16 + ((y + 3) % 4) * 4 + x, tm)

    def x_peer(d):
        return (z * 16 + y * 4 + (x + d) % 4, tm)

    def z_peer(d):
        there = (zall + d) % 8
        return (there % 4 * 16 + y * 4 + x, there // 4 * 2 + core)

    def t_peer(d):
        there = (t + d) % 8
        return (z * 16 + there // 2 * 4 + x, zh * 2 + there % 2)

    mate = z + 1 - 2 * (z % 2)
    zs = [z, mate, 3 - z, 3 - mate]
    spots = [(zs[k], xh) for k in range(4) for xh in (0, 1)]

    loads = [
        pltpu.make_async_copy(src, dst, local_sem.at[n])
        for n, (src, dst) in enumerate(((spec_ref, spec), (qual_ref, qown), (tab_hbm, tab)))
    ]
    for copy in loads:
        copy.start()
    barrier = pltpu.get_barrier_semaphore()
    greet = [(zt * 16 + y * 4 + 2 * xh + par, zh * 2 + x // 2) for zt, xh in spots]
    greet += [x_peer(d) for d in (1, 2, 3)]
    greet += [z_peer(d) for d in range(1, 8)]
    greet += [t_peer(d) for d in range(1, 8)]
    for there in greet:
        pl.semaphore_signal(barrier, inc=1, device_id=there, device_id_type=MESH)
    pl.semaphore_wait(barrier, len(greet))

    def remote(src, dst, ssem, rsem, there):
        return pltpu.make_async_remote_copy(
            src_ref=src, dst_ref=dst, send_sem=ssem, recv_sem=rsem, device_id=there, device_id_type=MESH
        )

    def send(src, dst, out_sem, in_sem, there):
        remote(src, dst, send_sem.at[out_sem], recv_sem.at[in_sem], there).start()

    def received(ref, in_sem):
        remote(ref, ref, send_sem.at[0], recv_sem.at[in_sem], sib).wait_recv()

    def gone(ref, sem):
        remote(ref, ref, sem, recv_sem.at[0], sib).wait_send()

    landings = [
        (2 * zt + low, (zt * 16 + y * 4 + low + 2 * core, zh * 2 + (x + low + 1 + core) % 2)) for zt, low in spots
    ]
    home = z * 2 + x // 2
    first_hop = [
        remote(lvown.at[i], lvin.at[home], row_sem.at[0], row_sem.at[1], there) for i, there in landings
    ]
    for i, there in landings:
        for q in range(4):
            src = spec_ref.at[:, i, :, q * 256 : (q + 1) * 256]
            dst = g.at[home, y * 2 + x % 2, q]
            first_hop.append(remote(src, dst, own_send.at[0], own_recv.at[home, q], there))
    for copy in first_hop[8:24]:
        copy.start()
    loads[0].wait()

    def measure(i, carry):
        re = spec[0, i].astype(F32)
        im = spec[1, i].astype(F32)
        lvown[i] = jnp.sum(jnp.sqrt(re * re + im * im), axis=0, keepdims=True)
        return carry

    lax.fori_loop(0, 8, measure, 0)
    for copy in first_hop[:8]:
        copy.start()
    for copy in first_hop[24:]:
        copy.start()
    loads[1].wait()
    send(qown, qbuf, 0, 0, sib)

    acc[...] = jnp.zeros_like(acc)
    w[NEED] = jnp.zeros_like(w[NEED])

    def hop(gi, m, q, kind, there):
        block = g.at[gi, m, q]
        arrival = gsib.at[gi] if kind == 3 else grecv.at[gi, m // 2, q]
        return remote(block, block, gsend.at[kind], arrival, there)

    def needs(at):
        return at, jnp.minimum(at + 2, 3)

    def upward(at, relay):
        lone = needs(at)
        return jnp.where(relay, jnp.where(at == 3, 0, at), lone[0]), jnp.where(relay, 3, lone[1])

    def downward(at, relay):
        lone = needs(at)
        return jnp.where(relay, jnp.maximum(at - 1, 0), lone[0]), jnp.where(relay, 3, lone[1])

    above, below, beyond = (y + 1) % 4, (y + 3) % 4, (y + 2) % 4
    mine = needs(y)

    def group_of(n):
        k = n // 2
        zt = jnp.where(k == 0, zs[0], jnp.where(k == 1, zs[1], jnp.where(k == 2, zs[2], zs[3])))
        return zt * 2 + n % 2

    def whitened(gi, m, tile):
        cols = tile_at(tile)
        half = tile_at(tile % 2)
        re = g[gi, m, tile // 2, 0, :, half].astype(F32)
        im = g[gi, m, tile // 2, 1, :, half].astype(F32)
        factor = use_ref[:, cols] / (jnp.sqrt(re * re + im * im) + add_ref[:, cols])
        return (re * factor).astype(BF), (im * factor).astype(BF)

    def within(q, span):
        return (q >= span[0]) & (q <= span[1])

    def start_if(wanted, *args):
        @pl.when(wanted)
        def _():
            hop(*args).start()

    def own(n):
        gi = group_of(n)
        m = y * 2 + par
        even = n % 2 == 0

        def one(q, carry):
            block = g.at[gi, m, q]
            remote(block, block, own_send.at[0], own_recv.at[gi, q], sib).wait_recv()

            @pl.when(n >= RAW)
            def _():
                for h in range(2):
                    re, im = whitened(gi, m, q * 2 + h)
                    g[gi, m, q, 0, :, h * TILE : (h + 1) * TILE] = re
                    g[gi, m, q, 1, :, h * TILE : (h + 1) * TILE] = im

            start_if(within(q, upward(above, even)), gi, m, q, 0, up)
            start_if(within(q, downward(below, jnp.logical_not(even))), gi, m, q, 1, down)
            start_if(within(q, mine), gi, m, q, 3, sib)
            return carry

        lax.fori_loop(0, 4, one, 0)

    def relay(gi, m, span, passed, there):
        def one(q, carry):
            hop(gi, m, q, 0, sib).wait_recv()
            start_if(within(q, passed), gi, m, q, 2, there)
            start_if(within(q, mine), gi, m, q, 3, sib)
            return carry

        lax.fori_loop(span[0], span[1] + 1, one, 0)

    def near(n):
        gi = group_of(n)
        even = n % 2 == 0
        lone = needs(above)
        passed = jnp.where(even, lone[0], 4), lone[1]
        relay(gi, below * 2 + par, upward(y, even), passed, up)
        lone = needs(below)
        passed = jnp.where(even, 4, lone[0]), lone[1]
        relay(gi, above * 2 + par, downward(y, jnp.logical_not(even)), passed, down)

    def far(n):
        relay(group_of(n), beyond * 2 + par, mine, (4, 4), up)

    lane = lax.broadcasted_iota(jnp.int32, (FB, TILE), 1)

    def compute(n):
        gi = group_of(n)
        count = mine[1] - mine[0] + 1
        for size in (1, 2, 3):

            @pl.when(count == size)
            def _(size=size):
                block = g.at[gi, pl.ds(0, size)]
                remote(block, block, gsend.at[3], gsib.at[gi], sib).wait_recv()


        @pl.when(n < RAW)
        def _():
            def whiten(m, carry):
                for a in range(NEED):
                    re, im = whitened(gi, m, jnp.minimum(t + a, 7))
                    w[a, 0, m] = jnp.where(t + a < 8, re, jnp.zeros_like(re))
                    w[a, 1, m] = jnp.where(t + a < 8, im, jnp.zeros_like(im))
                return carry

            lax.fori_loop(0, 8, whiten, 0, unroll=4)

        @pl.when(n >= RAW)
        def _():
            for a in range(NEED):
                tile = jnp.minimum(t + a, 7)
                for part in range(2):
                    value = g[gi, :, tile // 2, part, :, tile_at(tile % 2)]
                    w[a, part] = jnp.where(t + a < 8, value, jnp.zeros_like(value))

        def cross(m, carry):
            rows = pl.ds(pl.multiple_of(m * FB, FB), FB)
            own_re = w[0, 0, m].astype(F32)
            own_im = w[0, 1, m].astype(F32)
            for j in range(NOFF):
                whole = off_ref[j] // 8
                rest = off_ref[j] % 8 * 16
                keep = lane >= rest
                back = (TILE - rest) % TILE
                far_re = jnp.where(keep, w[whole, 0, m].astype(F32), w[whole + 1, 0, m].astype(F32))
                far_im = jnp.where(keep, w[whole, 1, m].astype(F32), w[whole + 1, 1, m].astype(F32))
                far_re = pltpu.roll(far_re, back, 1)
                far_im = pltpu.roll(far_im, back, 1)
                xmat[rows, j * TILE : (j + 1) * TILE] = (own_re * far_re + own_im * far_im).astype(BF)
                xmat[rows, 512 + j * TILE : 512 + (j + 1) * TILE] = (own_im * far_re - own_re * far_im).astype(BF)
            return carry

        lax.fori_loop(0, 8, cross, 0, unroll=8)
        acc[...] += jnp.dot(tab[gi], xmat[...], preferred_element_type=F32)

    for n in range(4):
        own(n)
    near(0)
    near(1)
    near(2)
    remote(lvin, lvin, row_sem.at[0], row_sem.at[1], sib).wait_recv()
    part = lvin[0]
    for k in range(1, 8):
        part = part + lvin[k]
    lvall[t] = part
    for d in range(1, 8):
        send(lvall.at[t], lvall.at[t], 1, 1, t_peer(d))
    near(3)
    for n in range(4):
        far(n)
    received(qbuf, 0)
    row = pl.ds(2 * z + x % 2, 1)
    use_ref[...] = jnp.where(x // 2 == core, qown[row], qbuf[row]).astype(F32)
    received(lvall.at[pl.ds(0, 7)], 1)
    level = lvall[0]
    for n in range(1, 8):
        level = level + lvall[n]
    add_ref[...] = 0.5 * (level / F + 1e-05)
    loads[2].wait()

    def turn(i, carry):
        @pl.when(i < 4)
        def _():
            own(i + 4)

        @pl.when((i >= 1) & (i < 5))
        def _():
            near(i + 3)

        @pl.when((i >= 2) & (i < 6))
        def _():
            far(i + 2)

        compute(i)
        return carry

    lax.fori_loop(0, 8, turn, 0)

    scale = 1.0 / math.sqrt(F)

    def phases(j):
        left = tile_at(j)
        right = tile_at(j + NOFF)
        a = acc[:HALF, left]
        b = acc[HALF:, right]
        c = acc[HALF:, left]
        d = acc[:HALF, right]
        pos_r = (a - b) * scale
        neg_r = (a + b) * scale
        pos_q = (d + c) * scale
        neg_q = (d - c) * scale
        power = (pos_r * pos_r + pos_q * pos_q) + (neg_r * neg_r + neg_q * neg_q)
        mean = jnp.sum(power, axis=0, keepdims=True) / LAGS
        floor = 0.25 * (mean + 1e-06)

        def halves(value):
            rows = value.reshape(8, 2, 8, TILE)
            return [rows[:, h].reshape(64, TILE) for h in range(2)]

        return floor, ((halves(pos_r), halves(pos_q)), (halves(neg_r), halves(neg_q)))

    def phasors(real, imag, floor):
        depth = jnp.sqrt((real * real + imag * imag) + floor)
        return real, real / depth, imag / depth

    def keep_pair(found, s, k):
        floor, values = found
        for h in range(2):
            pair[h, s, k, :64] = values[s][0][h]
            pair[h, s, k, 64:128] = values[s][1][h]
            pair[h, s, k, 128:] = jnp.broadcast_to(floor, (8, TILE))

    def keep_full(found, s, k):
        floor, values = found
        for h in range(2):
            for part, value in enumerate(phasors(values[s][0][h], values[s][1][h], floor)):
                p[h, s, k, part] = value

    def opened(h, n):
        return phasors(ring[h, n, :64], ring[h, n, 64:128], ring[h, n, 128:129])

    right, left, across = (x + 1) % 4, (x + 3) % 4, (x + 2) % 4

    def across_out(h):
        send(pair.at[h, 0, 0], ring.at[h, 0], 2, 2 + 6 * h, x_peer(1))
        send(pair.at[h, 1, 0], ring.at[h, 1], 2, 3 + 6 * h, x_peer(3))

    def plain_out(h):
        send(pair.at[h, 1, 1], ring.at[h, 2], 2, 4 + 6 * h, x_peer(1))
        send(pair.at[h, 0, 1], ring.at[h, 3], 2, 5 + 6 * h, x_peer(3))

    def both_out(h):
        for s in range(2):
            received(ring.at[h, s], 2 + 6 * h + s)
            for part, value in enumerate(opened(h, s)):
                ringsum[h, s, part] = value + p[h, s, 1, part]
            send(ringsum.at[h, s], ringin.at[h, s], 3, 6 + 6 * h + s, x_peer(3 if s else 1))

    def lag_rows(where):
        return pl.ds(pl.multiple_of(where * 8, 8), 8)

    def z_out(h):
        for s in range(2):
            received(ring.at[h, 3 - s], 5 + 6 * h - s)
            received(ringin.at[h, s], 6 + 6 * h + s)
            for part, value in enumerate(opened(h, 3 - s)):
                zacc[h, s, part] = (p[h, s, 0, part] + value) + ringin[h, s, part]
        for d in (4, 3, 5, 2, 6, 1, 7):
            send(zacc.at[h, :, :, lag_rows((zall + d) % 8)], zbuf.at[h, d - 1], 4 + h, 14 + h, z_peer(d))

    def z_in(h):
        received(zbuf.at[h], 14 + h)
        total = zacc[h, :, :, lag_rows(zall)]
        for d in range(7):
            total = total + zbuf[h, d]
        linear = total[:, 0] / WINDOWS
        real = total[:, 1] / WINDOWS
        imag = total[:, 2] / WINDOWS
        st[h, t] = linear * (real * real + imag * imag)
        for d in range(1, 8):
            send(st.at[h, t], st.at[h, t], 6, 16 + h, t_peer(d))

    found = phases(across)
    keep_pair(found, 0, 0)
    keep_pair(found, 1, 0)
    across_out(0)
    onward = phases(right)
    keep_pair(onward, 1, 1)
    back = phases(left)
    keep_pair(back, 0, 1)
    plain_out(0)
    across_out(1)
    keep_full(onward, 0, 1)
    keep_full(back, 1, 1)
    found = phases(x)
    keep_full(found, 0, 0)
    keep_full(found, 1, 0)
    both_out(0)
    plain_out(1)
    both_out(1)
    z_out(0)
    z_out(1)
    z_in(0)
    z_in(1)

    for h in range(2):
        received(st.at[h, pl.ds(0, 7)], 16 + h)
    shift = off_ref[x]
    whole = shift // 8
    rest = shift % 8 * 16
    wide = lax.broadcasted_iota(jnp.int32, (32, TILE), 1)

    def stack(tile):
        return jnp.concatenate([st[h, tile, s] for s in range(2) for h in range(2)], axis=0)

    pieces = []
    for n in range(4):
        tile = 2 * n + y // 2
        first = tile - whole
        a = jnp.where(first >= 0, stack(jnp.maximum(first, 0)), 0.0)
        b = jnp.where(first >= 1, stack(jnp.maximum(first - 1, 0)), 0.0)
        rev = pltpu.roll(jnp.where(wide < TILE - rest, a, b), rest, 1)
        ahead = stack(tile)
        pieces.append(ahead[:16] + rev[16:])
        pieces.append(ahead[16:] + rev[:16])
    tbuf[...] = jnp.concatenate(pieces, axis=0).T

    def channel_rows(where):
        return pl.ds(pl.multiple_of(y % 2 * 64 + where * 16, 16), 16)

    for d in (1, 2, 3):
        send(tbuf.at[channel_rows((x + d) % 4)], jbuf.at[x], 7, 18, x_peer(d))
    jbuf[x] = tbuf[channel_rows(x)]
    received(jbuf.at[pl.ds(0, 3)], 18)
    group = lax.broadcasted_iota(jnp.int32, (16, TILE), 1) // 32
    for n in range(4):
        merged = jnp.zeros((16, TILE), F32)
        for j in range(NOFF):
            merged = jnp.where(group == j, pltpu.roll(jbuf[j], (32 * (j - n)) % TILE, 1), merged)
        mbuf[n] = merged
    for d in (4, 3, 5, 2, 6, 1, 7):
        send(mbuf.at[(zall + d) % 4], rbuf.at[zall], 8, 19, z_peer(d))
    rbuf[zall] = mbuf[zall % 4]
    received(rbuf.at[pl.ds(0, 7)], 19)
    spot = lax.broadcasted_iota(jnp.int32, (16, TILE), 1)
    span = spot // 16
    for j in range(NOFF):
        for s in range(2):
            merged = jnp.zeros((16, TILE), F32)
            for n in range(8):
                at = 7 - n if s else n
                merged = jnp.where(span == at, pltpu.roll(rbuf[n], (16 * at - 32 * j - 16 * s) % TILE, 1), merged)
            if s:
                for bit in (1, 2, 4, 8):
                    merged = jnp.where(
                        spot // bit % 2 == 1, pltpu.roll(merged, bit, 1), pltpu.roll(merged, TILE - bit, 1)
                    )
            out_ref[:, j, (1 - s) * HALF : (2 - s) * HALF] = merged

    gone(lvown, row_sem.at[0])
    gone(g.at[0], own_send.at[0])
    gone(qown, send_sem.at[0])
    gone(lvall.at[pl.ds(0, 7)], send_sem.at[1])
    gone(ring, send_sem.at[2])
    gone(ringin, send_sem.at[3])
    for h in range(2):
        gone(zbuf.at[h], send_sem.at[4 + h])
    gone(st.at[:, pl.ds(0, 7)], send_sem.at[6])
    gone(jbuf.at[pl.ds(0, 3)], send_sem.at[7])
    gone(rbuf.at[pl.ds(0, 7)], send_sem.at[8])
    width = (3, 3, 2, 1)
    for at in range(4):
        ahead, behind = (at + 1) % 4, (at + 3) % 4
        upper = (4, 3, 2, 4)[ahead]
        lower = (4, 4, 3, 2)[behind]

        @pl.when(y == at)
        def _(at=at, ahead=ahead, behind=behind, upper=upper, lower=lower):
            gone(g.at[0, pl.ds(0, upper + width[ahead])], gsend.at[0])
            gone(g.at[0, pl.ds(0, lower + width[behind])], gsend.at[1])
            gone(g.at[0, pl.ds(0, width[ahead] + width[behind])], gsend.at[2])
            gone(g.at[pl.ds(0, width[at])], gsend.at[3])


def whole_window(offsets, spectra, quality, table):
    vmem = pl.BlockSpec(memory_space=pltpu.VMEM)
    return pl.pallas_call(
        window_kernel,
        name="whole_window",
        out_shape=jax.ShapeDtypeStruct((16, NOFF, LAGS), F32),
        in_specs=[pl.BlockSpec(memory_space=pltpu.SMEM)] + [pl.BlockSpec(memory_space=pl.ANY)] * 3,
        out_specs=vmem,
        scratch_shapes=[
            pltpu.VMEM((2, 8, FB, NCH), BF),
            pltpu.VMEM((8, NCH), jnp.int32),
            pltpu.VMEM((8, NCH), jnp.int32),
            pltpu.VMEM((8, 2 * HALF, GROUP), BF),
            pltpu.VMEM((8, 8, 4, 2, FB, 256), BF),
            pltpu.VMEM((8, 1, NCH), F32),
            pltpu.VMEM((8, 1, NCH), F32),
            pltpu.VMEM((8, 1, NCH), F32),
            pltpu.VMEM((1, NCH), F32),
            pltpu.VMEM((1, NCH), F32),
            pltpu.VMEM((NEED + 1, 2, 8, FB, TILE), BF),
            pltpu.VMEM((GROUP, 2 * NOFF * TILE), BF),
            pltpu.VMEM((2 * HALF, 2 * NOFF * TILE), F32),
            pltpu.VMEM((2, 2, 2, 3, 64, TILE), F32),
            pltpu.VMEM((2, 2, 2, 136, TILE), F32),
            pltpu.VMEM((2, 4, 136, TILE), F32),
            pltpu.VMEM((2, 2, 3, 64, TILE), F32),
            pltpu.VMEM((2, 2, 3, 64, TILE), F32),
            pltpu.VMEM((2, 2, 3, 64, TILE), F32),
            pltpu.VMEM((2, 7, 2, 3, 8, TILE), F32),
            pltpu.VMEM((2, 8, 2, 8, TILE), F32),
            pltpu.VMEM((TILE, TILE), F32),
            pltpu.VMEM((NOFF, 16, TILE), F32),
            pltpu.VMEM((4, 16, TILE), F32),
            pltpu.VMEM((8, 16, TILE), F32),
            pltpu.SemaphoreType.DMA((3,)),
            pltpu.SemaphoreType.DMA((8, 4)),
            pltpu.SemaphoreType.DMA((1,)),
            pltpu.SemaphoreType.DMA((2,)),
            pltpu.SemaphoreType.DMA((4,)),
            pltpu.SemaphoreType.DMA((8, 4, 4)),
            pltpu.SemaphoreType.DMA((8,)),
            pltpu.SemaphoreType.DMA((9,)),
            pltpu.SemaphoreType.DMA((20,)),
        ],
        compiler_params=pltpu.CompilerParams(collective_id=0, has_side_effects=True),
    )(offsets, spectra, quality, table)


def shards(spectra, quality, offsets):
    table = jnp.asarray(half_table()).astype(BF)
    return whole_window(offsets, spectra, quality, table)


def solution(mesh):
    return jax.shard_map(
        shards,
        mesh=mesh,
        in_specs=(P(None, "tm", "chan", None), P("tm", None), P()),
        out_specs=P("chan", None, None),
        check_vma=False,
    )
```

```python
import math

import jax
import jax.numpy as jnp
import numpy as np
from jax import lax
from jax.experimental import pallas as pl
from jax.experimental.pallas import tpu as pltpu
from jax.sharding import PartitionSpec as P

MESH = pl.DeviceIdType.MESH
F = 2048
LAGS = 256
HALF = 128
NOFF = 4
WINDOWS = 32
NCH = 1024
TILE = 128
FB = 32
NEED = 5
RAW = 4
GROUP = 256
BF = jnp.bfloat16
F32 = jnp.float32


def place():
    chan = lax.axis_index("chan")
    tm = lax.axis_index("tm")
    return chan // 16, (chan // 4) % 4, chan % 4, tm // 2, tm % 2


def half_table():
    z, half, y, par, low = np.meshgrid(*(np.arange(n) for n in (4, 2, 4, 2, FB)), indexing="ij")
    freq = ((z * 16 + y * 4 + 2 * half + par) * FB + low).reshape(8, 1, GROUP).astype(np.int64)
    lag = (2 * np.arange(HALF, dtype=np.int64) + 1)[None, :, None]
    angle = ((freq * lag) % (4 * F)).astype(np.float64) * (2.0 * math.pi / (4 * F))
    return np.concatenate([np.cos(angle), np.sin(angle)], axis=1).astype(np.float32)


def tile_at(where):
    return pl.ds(pl.multiple_of(where * TILE, TILE), TILE)


def window_kernel(
    off_ref, spec_ref, qual_ref, tab_hbm, out_ref,
    spec, qown, qbuf, tab, g, lvown, lvin, lvall, add_ref, use_ref, w, xmat, acc, p,
    pair, ring, ringsum, ringin, zacc, zbuf, st, tbuf, jbuf, mbuf, rbuf,
    local_sem, own_send, row_sem, gsend, grecv, gsib, send_sem, recv_sem,
):
    z, y, x, zh, core = place()
    chan = z * 16 + y * 4 + x
    tm = zh * 2 + core
    sib = (chan, zh * 2 + 1 - core)
    t = y * 2 + core
    zall = zh * 4 + z
    par = (core + x + 1 + x // 2) % 2
    up = (z * 16 + ((y + 1) % 4) * 4 + x, tm)
    down = (z * 16 + ((y + 3) % 4) * 4 + x, tm)

    def x_peer(d):
        return (z * 16 + y * 4 + (x + d) % 4, tm)

    def z_peer(d):
        there = (zall + d) % 8
        return (there % 4 * 16 + y * 4 + x, there // 4 * 2 + core)

    def t_peer(d):
        there = (t + d) % 8
        return (z * 16 + there // 2 * 4 + x, zh * 2 + there % 2)

    mate = z + 1 - 2 * (z % 2)
    zs = [z, mate, 3 - z, 3 - mate]
    spots = [(zs[k], xh) for k in range(4) for xh in (0, 1)]

    loads = [
        pltpu.make_async_copy(src, dst, local_sem.at[n])
        for n, (src, dst) in enumerate(((spec_ref, spec), (qual_ref, qown), (tab_hbm, tab)))
    ]
    for copy in loads:
        copy.start()
    barrier = pltpu.get_barrier_semaphore()
    greet = [(zt * 16 + y * 4 + 2 * xh + par, zh * 2 + x // 2) for zt, xh in spots]
    greet += [x_peer(d) for d in (1, 2, 3)]
    greet += [z_peer(d) for d in range(1, 8)]
    greet += [t_peer(d) for d in range(1, 8)]
    for there in greet:
        pl.semaphore_signal(barrier, inc=1, device_id=there, device_id_type=MESH)
    pl.semaphore_wait(barrier, len(greet))

    def remote(src, dst, ssem, rsem, there):
        return pltpu.make_async_remote_copy(
            src_ref=src, dst_ref=dst, send_sem=ssem, recv_sem=rsem, device_id=there, device_id_type=MESH
        )

    def send(src, dst, out_sem, in_sem, there):
        remote(src, dst, send_sem.at[out_sem], recv_sem.at[in_sem], there).start()

    def received(ref, in_sem):
        remote(ref, ref, send_sem.at[0], recv_sem.at[in_sem], sib).wait_recv()

    def gone(ref, sem):
        remote(ref, ref, sem, recv_sem.at[0], sib).wait_send()

    landings = [
        (2 * zt + low, (zt * 16 + y * 4 + low + 2 * core, zh * 2 + (x + low + 1 + core) % 2)) for zt, low in spots
    ]
    home = z * 2 + x // 2
    first_hop = [
        remote(lvown.at[i], lvin.at[home], row_sem.at[0], row_sem.at[1], there) for i, there in landings
    ]
    for i, there in landings:
        for q in range(4):
            src = spec_ref.at[:, i, :, q * 256 : (q + 1) * 256]
            dst = g.at[home, y * 2 + x % 2, q]
            first_hop.append(remote(src, dst, own_send.at[0], grecv.at[home, y, q], there))
    for copy in first_hop[8:24]:
        copy.start()
    loads[0].wait()

    def measure(i, carry):
        re = spec[0, i].astype(F32)
        im = spec[1, i].astype(F32)
        lvown[i] = jnp.sum(jnp.sqrt(re * re + im * im), axis=0, keepdims=True)
        return carry

    lax.fori_loop(0, 8, measure, 0)
    for copy in first_hop[:8]:
        copy.start()
    for copy in first_hop[24:]:
        copy.start()
    loads[1].wait()
    send(qown, qbuf, 0, 0, sib)

    acc[...] = jnp.zeros_like(acc)
    w[NEED] = jnp.zeros_like(w[NEED])

    def hop(gi, m, q, kind, there):
        block = g.at[gi, m, q]
        arrival = gsib.at[gi] if kind == 3 else grecv.at[gi, m // 2, q]
        return remote(block, block, gsend.at[kind], arrival, there)

    def needs(at):
        return at, jnp.minimum(at + 2, 3)

    def upward(at, relay):
        lone = needs(at)
        return jnp.where(relay, jnp.where(at == 3, 0, at), lone[0]), jnp.where(relay, 3, lone[1])

    def downward(at, relay):
        lone = needs(at)
        return jnp.where(relay, jnp.maximum(at - 1, 0), lone[0]), jnp.where(relay, 3, lone[1])

    above, below, beyond = (y + 1) % 4, (y + 3) % 4, (y + 2) % 4
    mine = needs(y)

    def group_of(n):
        k = n // 2
        zt = jnp.where(k == 0, zs[0], jnp.where(k == 1, zs[1], jnp.where(k == 2, zs[2], zs[3])))
        return zt * 2 + n % 2

    def whitened(gi, m, tile):
        cols = tile_at(tile)
        half = tile_at(tile % 2)
        re = g[gi, m, tile // 2, 0, :, half].astype(F32)
        im = g[gi, m, tile // 2, 1, :, half].astype(F32)
        factor = use_ref[:, cols] / (jnp.sqrt(re * re + im * im) + add_ref[:, cols])
        return (re * factor).astype(BF), (im * factor).astype(BF)

    def within(q, span):
        return (q >= span[0]) & (q <= span[1])

    def start_if(wanted, *args):
        @pl.when(wanted)
        def _():
            hop(*args).start()

    def own(n):
        gi = group_of(n)
        m = y * 2 + par
        even = n % 2 == 0

        def one(q, carry):
            block = g.at[gi, m, q]
            remote(block, block, own_send.at[0], grecv.at[gi, y, q], sib).wait_recv()

            @pl.when(n >= RAW)
            def _():
                for h in range(2):
                    re, im = whitened(gi, m, q * 2 + h)
                    g[gi, m, q, 0, :, h * TILE : (h + 1) * TILE] = re
                    g[gi, m, q, 1, :, h * TILE : (h + 1) * TILE] = im

            start_if(within(q, upward(above, even)), gi, m, q, 0, up)
            start_if(within(q, downward(below, jnp.logical_not(even))), gi, m, q, 1, down)
            start_if(within(q, mine), gi, m, q, 3, sib)
            return carry

        lax.fori_loop(0, 4, one, 0)

    def relay(gi, m, span, passed, there):
        def one(q, carry):
            hop(gi, m, q, 0, sib).wait_recv()
            start_if(within(q, passed), gi, m, q, 2, there)
            start_if(within(q, mine), gi, m, q, 3, sib)
            return carry

        lax.fori_loop(span[0], span[1] + 1, one, 0)

    def near(n):
        gi = group_of(n)
        even = n % 2 == 0
        lone = needs(above)
        passed = jnp.where(even, lone[0], 4), lone[1]
        relay(gi, below * 2 + par, upward(y, even), passed, up)
        lone = needs(below)
        passed = jnp.where(even, 4, lone[0]), lone[1]
        relay(gi, above * 2 + par, downward(y, jnp.logical_not(even)), passed, down)

    def far(n):
        relay(group_of(n), beyond * 2 + par, mine, (4, 4), up)

    lane = lax.broadcasted_iota(jnp.int32, (FB, TILE), 1)

    def compute(n):
        gi = group_of(n)
        count = mine[1] - mine[0] + 1
        for size in (1, 2, 3):

            @pl.when(count == size)
            def _(size=size):
                block = g.at[gi, pl.ds(0, size)]
                remote(block, block, gsend.at[3], gsib.at[gi], sib).wait_recv()


        @pl.when(n < RAW)
        def _():
            def whiten(m, carry):
                for a in range(NEED):
                    re, im = whitened(gi, m, jnp.minimum(t + a, 7))
                    w[a, 0, m] = jnp.where(t + a < 8, re, jnp.zeros_like(re))
                    w[a, 1, m] = jnp.where(t + a < 8, im, jnp.zeros_like(im))
                return carry

            lax.fori_loop(0, 8, whiten, 0, unroll=4)

        @pl.when(n >= RAW)
        def _():
            for a in range(NEED):
                tile = jnp.minimum(t + a, 7)
                for part in range(2):
                    value = g[gi, :, tile // 2, part, :, tile_at(tile % 2)]
                    w[a, part] = jnp.where(t + a < 8, value, jnp.zeros_like(value))

        def cross(m, carry):
            rows = pl.ds(pl.multiple_of(m * FB, FB), FB)
            own_re = w[0, 0, m].astype(F32)
            own_im = w[0, 1, m].astype(F32)
            for j in range(NOFF):
                whole = off_ref[j] // 8
                rest = off_ref[j] % 8 * 16
                keep = lane >= rest
                back = (TILE - rest) % TILE
                far_re = jnp.where(keep, w[whole, 0, m].astype(F32), w[whole + 1, 0, m].astype(F32))
                far_im = jnp.where(keep, w[whole, 1, m].astype(F32), w[whole + 1, 1, m].astype(F32))
                far_re = pltpu.roll(far_re, back, 1)
                far_im = pltpu.roll(far_im, back, 1)
                xmat[rows, j * TILE : (j + 1) * TILE] = (own_re * far_re + own_im * far_im).astype(BF)
                xmat[rows, 512 + j * TILE : 512 + (j + 1) * TILE] = (own_im * far_re - own_re * far_im).astype(BF)
            return carry

        lax.fori_loop(0, 8, cross, 0, unroll=8)
        acc[...] += jnp.dot(tab[gi], xmat[...], preferred_element_type=F32)

    for n in range(4):
        own(n)
    near(0)
    near(1)
    near(2)
    remote(lvin, lvin, row_sem.at[0], row_sem.at[1], sib).wait_recv()
    part = lvin[0]
    for k in range(1, 8):
        part = part + lvin[k]
    lvall[t] = part
    for d in range(1, 8):
        send(lvall.at[t], lvall.at[t], 1, 1, t_peer(d))
    near(3)
    for n in range(4):
        far(n)
    received(qbuf, 0)
    row = pl.ds(2 * z + x % 2, 1)
    use_ref[...] = jnp.where(x // 2 == core, qown[row], qbuf[row]).astype(F32)
    received(lvall.at[pl.ds(0, 7)], 1)
    level = lvall[0]
    for n in range(1, 8):
        level = level + lvall[n]
    add_ref[...] = 0.5 * (level / F + 1e-05)
    loads[2].wait()

    def turn(i, carry):
        @pl.when(i < 4)
        def _():
            own(i + 4)

        @pl.when((i >= 1) & (i < 5))
        def _():
            near(i + 3)

        @pl.when((i >= 2) & (i < 6))
        def _():
            far(i + 2)

        compute(i)
        return carry

    lax.fori_loop(0, 8, turn, 0)

    scale = 1.0 / math.sqrt(F)

    def phases(j):
        left = tile_at(j)
        right = tile_at(j + NOFF)
        a = acc[:HALF, left]
        b = acc[HALF:, right]
        c = acc[HALF:, left]
        d = acc[:HALF, right]
        pos_r = (a - b) * scale
        neg_r = (a + b) * scale
        pos_q = (d + c) * scale
        neg_q = (d - c) * scale
        power = (pos_r * pos_r + pos_q * pos_q) + (neg_r * neg_r + neg_q * neg_q)
        mean = jnp.sum(power, axis=0, keepdims=True) / LAGS
        floor = 0.25 * (mean + 1e-06)

        def halves(value):
            rows = value.reshape(8, 2, 8, TILE)
            return [rows[:, h].reshape(64, TILE) for h in range(2)]

        return floor, ((halves(pos_r), halves(pos_q)), (halves(neg_r), halves(neg_q)))

    def phasors(real, imag, floor):
        depth = jnp.sqrt((real * real + imag * imag) + floor)
        return real, real / depth, imag / depth

    def keep_pair(found, s, k):
        floor, values = found
        for h in range(2):
            pair[h, s, k, :64] = values[s][0][h]
            pair[h, s, k, 64:128] = values[s][1][h]
            pair[h, s, k, 128:] = jnp.broadcast_to(floor, (8, TILE))

    def keep_full(found, s, k):
        floor, values = found
        for h in range(2):
            for part, value in enumerate(phasors(values[s][0][h], values[s][1][h], floor)):
                p[h, s, k, part] = value

    def opened(h, n):
        return phasors(ring[h, n, :64], ring[h, n, 64:128], ring[h, n, 128:129])

    right, left, across = (x + 1) % 4, (x + 3) % 4, (x + 2) % 4

    def across_out(h):
        send(pair.at[h, 0, 0], ring.at[h, 0], 2, 2 + 6 * h, x_peer(1))
        send(pair.at[h, 1, 0], ring.at[h, 1], 2, 3 + 6 * h, x_peer(3))

    def plain_out(h):
        send(pair.at[h, 1, 1], ring.at[h, 2], 2, 4 + 6 * h, x_peer(1))
        send(pair.at[h, 0, 1], ring.at[h, 3], 2, 5 + 6 * h, x_peer(3))

    def both_out(h):
        for s in range(2):
            received(ring.at[h, s], 2 + 6 * h + s)
            for part, value in enumerate(opened(h, s)):
                ringsum[h, s, part] = value + p[h, s, 1, part]
            send(ringsum.at[h, s], ringin.at[h, s], 3, 6 + 6 * h + s, x_peer(3 if s else 1))

    def lag_rows(where):
        return pl.ds(pl.multiple_of(where * 8, 8), 8)

    def z_out(h):
        for s in range(2):
            received(ring.at[h, 3 - s], 5 + 6 * h - s)
            received(ringin.at[h, s], 6 + 6 * h + s)
            for part, value in enumerate(opened(h, 3 - s)):
                zacc[h, s, part] = (p[h, s, 0, part] + value) + ringin[h, s, part]
        for d in (4, 3, 5, 2, 6, 1, 7):
            send(zacc.at[h, :, :, lag_rows((zall + d) % 8)], zbuf.at[h, d - 1], 4 + h, 14 + h, z_peer(d))

    def z_in(h):
        received(zbuf.at[h], 14 + h)
        total = zacc[h, :, :, lag_rows(zall)]
        for d in range(7):
            total = total + zbuf[h, d]
        linear = total[:, 0] / WINDOWS
        real = total[:, 1] / WINDOWS
        imag = total[:, 2] / WINDOWS
        st[h, t] = linear * (real * real + imag * imag)
        for d in range(1, 8):
            send(st.at[h, t], st.at[h, t], 6, 16 + h, t_peer(d))

    found = phases(across)
    keep_pair(found, 0, 0)
    keep_pair(found, 1, 0)
    across_out(0)
    onward = phases(right)
    keep_pair(onward, 1, 1)
    back = phases(left)
    keep_pair(back, 0, 1)
    plain_out(0)
    across_out(1)
    keep_full(onward, 0, 1)
    keep_full(back, 1, 1)
    both_out(0)
    plain_out(1)
    found = phases(x)
    keep_full(found, 0, 0)
    keep_full(found, 1, 0)
    both_out(1)
    z_out(0)
    z_out(1)
    z_in(0)
    z_in(1)

    for h in range(2):
        received(st.at[h, pl.ds(0, 7)], 16 + h)
    shift = off_ref[x]
    whole = shift // 8
    rest = shift % 8 * 16
    wide = lax.broadcasted_iota(jnp.int32, (32, TILE), 1)

    def stack(tile):
        return jnp.concatenate([st[h, tile, s] for s in range(2) for h in range(2)], axis=0)

    pieces = []
    for n in range(4):
        tile = 2 * n + y // 2
        first = tile - whole
        a = jnp.where(first >= 0, stack(jnp.maximum(first, 0)), 0.0)
        b = jnp.where(first >= 1, stack(jnp.maximum(first - 1, 0)), 0.0)
        rev = pltpu.roll(jnp.where(wide < TILE - rest, a, b), rest, 1)
        ahead = stack(tile)
        pieces.append(ahead[:16] + rev[16:])
        pieces.append(ahead[16:] + rev[:16])
    tbuf[...] = jnp.concatenate(pieces, axis=0).T

    def channel_rows(where):
        return pl.ds(pl.multiple_of(y % 2 * 64 + where * 16, 16), 16)

    for d in (1, 2, 3):
        send(tbuf.at[channel_rows((x + d) % 4)], jbuf.at[x], 7, 18, x_peer(d))
    jbuf[x] = tbuf[channel_rows(x)]
    received(jbuf.at[pl.ds(0, 3)], 18)
    group = lax.broadcasted_iota(jnp.int32, (16, TILE), 1) // 32
    for n in range(4):
        merged = jnp.zeros((16, TILE), F32)
        for j in range(NOFF):
            merged = jnp.where(group == j, pltpu.roll(jbuf[j], (32 * (j - n)) % TILE, 1), merged)
        mbuf[n] = merged
    for d in (4, 3, 5, 2, 6, 1, 7):
        send(mbuf.at[(zall + d) % 4], rbuf.at[zall], 8, 19, z_peer(d))
    rbuf[zall] = mbuf[zall % 4]
    received(rbuf.at[pl.ds(0, 7)], 19)
    spot = lax.broadcasted_iota(jnp.int32, (16, TILE), 1)
    span = spot // 16
    for j in range(NOFF):
        for s in range(2):
            merged = jnp.zeros((16, TILE), F32)
            for n in range(8):
                at = 7 - n if s else n
                merged = jnp.where(span == at, pltpu.roll(rbuf[n], (16 * at - 32 * j - 16 * s) % TILE, 1), merged)
            if s:
                for bit in (1, 2, 4, 8):
                    merged = jnp.where(
                        spot // bit % 2 == 1, pltpu.roll(merged, bit, 1), pltpu.roll(merged, TILE - bit, 1)
                    )
            out_ref[1 - s, j] = merged

    gone(lvown, row_sem.at[0])
    gone(g.at[0], own_send.at[0])
    gone(qown, send_sem.at[0])
    gone(lvall.at[pl.ds(0, 7)], send_sem.at[1])
    gone(ring, send_sem.at[2])
    gone(ringin, send_sem.at[3])
    for h in range(2):
        gone(zbuf.at[h], send_sem.at[4 + h])
    gone(st.at[:, pl.ds(0, 7)], send_sem.at[6])
    gone(jbuf.at[pl.ds(0, 3)], send_sem.at[7])
    gone(rbuf.at[pl.ds(0, 7)], send_sem.at[8])
    width = (3, 3, 2, 1)
    for at in range(4):
        ahead, behind = (at + 1) % 4, (at + 3) % 4
        upper = (4, 3, 2, 4)[ahead]
        lower = (4, 4, 3, 2)[behind]

        @pl.when(y == at)
        def _(at=at, ahead=ahead, behind=behind, upper=upper, lower=lower):
            gone(g.at[0, pl.ds(0, upper + width[ahead])], gsend.at[0])
            gone(g.at[0, pl.ds(0, lower + width[behind])], gsend.at[1])
            gone(g.at[0, pl.ds(0, width[ahead] + width[behind])], gsend.at[2])
            gone(g.at[pl.ds(0, width[at])], gsend.at[3])


def whole_window(offsets, spectra, quality, table):
    vmem = pl.BlockSpec(memory_space=pltpu.VMEM)
    return pl.pallas_call(
        window_kernel,
        name="whole_window",
        out_shape=jax.ShapeDtypeStruct((2, NOFF, 16, HALF), F32),
        in_specs=[pl.BlockSpec(memory_space=pltpu.SMEM)] + [pl.BlockSpec(memory_space=pl.ANY)] * 3,
        out_specs=vmem,
        scratch_shapes=[
            pltpu.VMEM((2, 8, FB, NCH), BF),
            pltpu.VMEM((8, NCH), jnp.int32),
            pltpu.VMEM((8, NCH), jnp.int32),
            pltpu.VMEM((8, 2 * HALF, GROUP), BF),
            pltpu.VMEM((8, 8, 4, 2, FB, 256), BF),
            pltpu.VMEM((8, 1, NCH), F32),
            pltpu.VMEM((8, 1, NCH), F32),
            pltpu.VMEM((8, 1, NCH), F32),
            pltpu.VMEM((1, NCH), F32),
            pltpu.VMEM((1, NCH), F32),
            pltpu.VMEM((NEED + 1, 2, 8, FB, TILE), BF),
            pltpu.VMEM((GROUP, 2 * NOFF * TILE), BF),
            pltpu.VMEM((2 * HALF, 2 * NOFF * TILE), F32),
            pltpu.VMEM((2, 2, 2, 3, 64, TILE), F32),
            pltpu.VMEM((2, 2, 2, 136, TILE), F32),
            pltpu.VMEM((2, 4, 136, TILE), F32),
            pltpu.VMEM((2, 2, 3, 64, TILE), F32),
            pltpu.VMEM((2, 2, 3, 64, TILE), F32),
            pltpu.VMEM((2, 2, 3, 64, TILE), F32),
            pltpu.VMEM((2, 7, 2, 3, 8, TILE), F32),
            pltpu.VMEM((2, 8, 2, 8, TILE), F32),
            pltpu.VMEM((TILE, TILE), F32),
            pltpu.VMEM((NOFF, 16, TILE), F32),
            pltpu.VMEM((4, 16, TILE), F32),
            pltpu.VMEM((8, 16, TILE), F32),
            pltpu.SemaphoreType.DMA((3,)),
            pltpu.SemaphoreType.DMA((1,)),
            pltpu.SemaphoreType.DMA((2,)),
            pltpu.SemaphoreType.DMA((4,)),
            pltpu.SemaphoreType.DMA((8, 4, 4)),
            pltpu.SemaphoreType.DMA((8,)),
            pltpu.SemaphoreType.DMA((9,)),
            pltpu.SemaphoreType.DMA((20,)),
        ],
        compiler_params=pltpu.CompilerParams(collective_id=0, has_side_effects=True),
    )(offsets, spectra, quality, table)


def shards(spectra, quality, offsets):
    table = jnp.asarray(half_table()).astype(BF)
    halves = whole_window(offsets, spectra, quality, table)
    return jnp.transpose(halves, (2, 1, 0, 3)).reshape(16, NOFF, LAGS)


def solution(mesh):
    return jax.shard_map(
        shards,
        mesh=mesh,
        in_specs=(P(None, "tm", "chan", None), P("tm", None), P()),
        out_specs=P("chan", None, None),
        check_vma=False,
    )
```

```python
import math

import jax
import jax.numpy as jnp
import numpy as np
from jax import lax
from jax.experimental import pallas as pl
from jax.experimental.pallas import tpu as pltpu
from jax.sharding import PartitionSpec as P

MESH = pl.DeviceIdType.MESH
F = 2048
LAGS = 256
HALF = 128
NOFF = 4
WINDOWS = 32
NCH = 1024
TILE = 128
FB = 32
NEED = 5
RAW = 4
GROUP = 256
BF = jnp.bfloat16
F32 = jnp.float32


def place():
    chan = lax.axis_index("chan")
    tm = lax.axis_index("tm")
    return chan // 16, (chan // 4) % 4, chan % 4, tm // 2, tm % 2


def half_table():
    z, half, y, par, low = np.meshgrid(*(np.arange(n) for n in (4, 2, 4, 2, FB)), indexing="ij")
    freq = ((z * 16 + y * 4 + 2 * half + par) * FB + low).reshape(8, 1, GROUP).astype(np.int64)
    lag = (2 * np.arange(HALF, dtype=np.int64) + 1)[None, :, None]
    angle = ((freq * lag) % (4 * F)).astype(np.float64) * (2.0 * math.pi / (4 * F))
    return np.concatenate([np.cos(angle), np.sin(angle)], axis=1).astype(np.float32)


def tile_at(where):
    return pl.ds(pl.multiple_of(where * TILE, TILE), TILE)


def window_kernel(
    off_ref, spec_ref, qual_ref, tab_hbm, out_ref,
    spec, qown, qbuf, tab, g, lvown, lvin, lvall, add_ref, use_ref, w, xmat, acc, p,
    pair, ring, ringsum, ringin, zacc, zbuf, st, tbuf, jbuf, mbuf, rbuf,
    local_sem, own_send, row_sem, gsend, grecv, gsib, send_sem, recv_sem,
):
    z, y, x, zh, core = place()
    chan = z * 16 + y * 4 + x
    tm = zh * 2 + core
    sib = (chan, zh * 2 + 1 - core)
    t = y * 2 + core
    zall = zh * 4 + z
    par = (core + x + 1 + x // 2) % 2
    up = (z * 16 + ((y + 1) % 4) * 4 + x, tm)
    down = (z * 16 + ((y + 3) % 4) * 4 + x, tm)

    def x_peer(d):
        return (z * 16 + y * 4 + (x + d) % 4, tm)

    def z_peer(d):
        there = (zall + d) % 8
        return (there % 4 * 16 + y * 4 + x, there // 4 * 2 + core)

    def t_peer(d):
        there = (t + d) % 8
        return (z * 16 + there // 2 * 4 + x, zh * 2 + there % 2)

    mate = z + 1 - 2 * (z % 2)
    zs = [z, mate, 3 - z, 3 - mate]
    spots = [(zs[k], xh) for k in range(4) for xh in (0, 1)]

    loads = [
        pltpu.make_async_copy(src, dst, local_sem.at[n])
        for n, (src, dst) in enumerate(((spec_ref, spec), (qual_ref, qown), (tab_hbm, tab)))
    ]
    for copy in loads:
        copy.start()
    barrier = pltpu.get_barrier_semaphore()
    greet = [(zt * 16 + y * 4 + 2 * xh + par, zh * 2 + x // 2) for zt, xh in spots]
    greet += [x_peer(d) for d in (1, 2, 3)]
    greet += [z_peer(d) for d in range(1, 8)]
    greet += [t_peer(d) for d in range(1, 8)]
    for there in greet:
        pl.semaphore_signal(barrier, inc=1, device_id=there, device_id_type=MESH)
    pl.semaphore_wait(barrier, len(greet))

    def remote(src, dst, ssem, rsem, there):
        return pltpu.make_async_remote_copy(
            src_ref=src, dst_ref=dst, send_sem=ssem, recv_sem=rsem, device_id=there, device_id_type=MESH
        )

    def send(src, dst, out_sem, in_sem, there):
        remote(src, dst, send_sem.at[out_sem], recv_sem.at[in_sem], there).start()

    def received(ref, in_sem):
        remote(ref, ref, send_sem.at[0], recv_sem.at[in_sem], sib).wait_recv()

    def gone(ref, sem):
        remote(ref, ref, sem, recv_sem.at[0], sib).wait_send()

    landings = [
        (2 * zt + low, (zt * 16 + y * 4 + low + 2 * core, zh * 2 + (x + low + 1 + core) % 2)) for zt, low in spots
    ]
    home = z * 2 + x // 2
    first_hop = [
        remote(lvown.at[i], lvin.at[home], row_sem.at[0], row_sem.at[1], there) for i, there in landings
    ]
    for i, there in landings:
        for q in range(4):
            src = spec_ref.at[:, i, :, q * 256 : (q + 1) * 256]
            dst = g.at[home, y * 2 + x % 2, q]
            first_hop.append(remote(src, dst, own_send.at[0], grecv.at[home, y, q], there))
    for copy in first_hop[8:24]:
        copy.start()
    loads[0].wait()

    def measure(i, carry):
        re = spec[0, i].astype(F32)
        im = spec[1, i].astype(F32)
        lvown[i] = jnp.sum(jnp.sqrt(re * re + im * im), axis=0, keepdims=True)
        return carry

    lax.fori_loop(0, 8, measure, 0, unroll=4)
    for copy in first_hop[:8]:
        copy.start()
    for copy in first_hop[24:]:
        copy.start()
    loads[1].wait()
    send(qown, qbuf, 0, 0, sib)

    acc[...] = jnp.zeros_like(acc)
    w[NEED] = jnp.zeros_like(w[NEED])

    def hop(gi, m, q, kind, there):
        block = g.at[gi, m, q]
        arrival = gsib.at[gi] if kind == 3 else grecv.at[gi, m // 2, q]
        return remote(block, block, gsend.at[kind], arrival, there)

    def needs(at):
        return at, jnp.minimum(at + 2, 3)

    def upward(at, relay):
        lone = needs(at)
        return jnp.where(relay, jnp.where(at == 3, 0, at), lone[0]), jnp.where(relay, 3, lone[1])

    def downward(at, relay):
        lone = needs(at)
        return jnp.where(relay, jnp.maximum(at - 1, 0), lone[0]), jnp.where(relay, 3, lone[1])

    above, below, beyond = (y + 1) % 4, (y + 3) % 4, (y + 2) % 4
    mine = needs(y)

    def group_of(n):
        k = n // 2
        zt = jnp.where(k == 0, zs[0], jnp.where(k == 1, zs[1], jnp.where(k == 2, zs[2], zs[3])))
        return zt * 2 + n % 2

    def whitened(gi, m, tile):
        cols = tile_at(tile)
        half = tile_at(tile % 2)
        re = g[gi, m, tile // 2, 0, :, half].astype(F32)
        im = g[gi, m, tile // 2, 1, :, half].astype(F32)
        factor = use_ref[:, cols] / (jnp.sqrt(re * re + im * im) + add_ref[:, cols])
        return (re * factor).astype(BF), (im * factor).astype(BF)

    def within(q, span):
        return (q >= span[0]) & (q <= span[1])

    def start_if(wanted, *args):
        @pl.when(wanted)
        def _():
            hop(*args).start()

    def own(n):
        gi = group_of(n)
        m = y * 2 + par
        even = n % 2 == 0

        def one(q, carry):
            block = g.at[gi, m, q]
            remote(block, block, own_send.at[0], grecv.at[gi, y, q], sib).wait_recv()

            @pl.when(n >= RAW)
            def _():
                for h in range(2):
                    re, im = whitened(gi, m, q * 2 + h)
                    g[gi, m, q, 0, :, h * TILE : (h + 1) * TILE] = re
                    g[gi, m, q, 1, :, h * TILE : (h + 1) * TILE] = im

            start_if(within(q, upward(above, even)), gi, m, q, 0, up)
            start_if(within(q, downward(below, jnp.logical_not(even))), gi, m, q, 1, down)
            start_if(within(q, mine), gi, m, q, 3, sib)
            return carry

        lax.fori_loop(0, 4, one, 0)

    def relay(gi, m, span, passed, there):
        def one(q, carry):
            hop(gi, m, q, 0, sib).wait_recv()
            start_if(within(q, passed), gi, m, q, 2, there)
            start_if(within(q, mine), gi, m, q, 3, sib)
            return carry

        lax.fori_loop(span[0], span[1] + 1, one, 0)

    def near(n):
        gi = group_of(n)
        even = n % 2 == 0
        lone = needs(above)
        passed = jnp.where(even, lone[0], 4), lone[1]
        relay(gi, below * 2 + par, upward(y, even), passed, up)
        lone = needs(below)
        passed = jnp.where(even, 4, lone[0]), lone[1]
        relay(gi, above * 2 + par, downward(y, jnp.logical_not(even)), passed, down)

    def far(n):
        relay(group_of(n), beyond * 2 + par, mine, (4, 4), up)

    lane = lax.broadcasted_iota(jnp.int32, (FB, TILE), 1)

    def compute(n):
        gi = group_of(n)
        count = mine[1] - mine[0] + 1
        for size in (1, 2, 3):

            @pl.when(count == size)
            def _(size=size):
                block = g.at[gi, pl.ds(0, size)]
                remote(block, block, gsend.at[3], gsib.at[gi], sib).wait_recv()


        @pl.when(n < RAW)
        def _():
            def whiten(m, carry):
                for a in range(NEED):
                    re, im = whitened(gi, m, jnp.minimum(t + a, 7))
                    w[a, 0, m] = jnp.where(t + a < 8, re, jnp.zeros_like(re))
                    w[a, 1, m] = jnp.where(t + a < 8, im, jnp.zeros_like(im))
                return carry

            lax.fori_loop(0, 8, whiten, 0, unroll=8)

        @pl.when(n >= RAW)
        def _():
            for a in range(NEED):
                tile = jnp.minimum(t + a, 7)
                for part in range(2):
                    value = g[gi, :, tile // 2, part, :, tile_at(tile % 2)]
                    w[a, part] = jnp.where(t + a < 8, value, jnp.zeros_like(value))

        def cross(m, carry):
            rows = pl.ds(pl.multiple_of(m * FB, FB), FB)
            own_re = w[0, 0, m].astype(F32)
            own_im = w[0, 1, m].astype(F32)
            for j in range(NOFF):
                whole = off_ref[j] // 8
                rest = off_ref[j] % 8 * 16
                keep = lane >= rest
                back = (TILE - rest) % TILE
                far_re = jnp.where(keep, w[whole, 0, m].astype(F32), w[whole + 1, 0, m].astype(F32))
                far_im = jnp.where(keep, w[whole, 1, m].astype(F32), w[whole + 1, 1, m].astype(F32))
                far_re = pltpu.roll(far_re, back, 1)
                far_im = pltpu.roll(far_im, back, 1)
                xmat[rows, j * TILE : (j + 1) * TILE] = (own_re * far_re + own_im * far_im).astype(BF)
                xmat[rows, 512 + j * TILE : 512 + (j + 1) * TILE] = (own_im * far_re - own_re * far_im).astype(BF)
            return carry

        lax.fori_loop(0, 8, cross, 0, unroll=8)
        acc[...] += jnp.dot(tab[gi], xmat[...], preferred_element_type=F32)

    for n in range(4):
        own(n)
    near(0)
    near(1)
    near(2)
    remote(lvin, lvin, row_sem.at[0], row_sem.at[1], sib).wait_recv()
    part = lvin[0]
    for k in range(1, 8):
        part = part + lvin[k]
    lvall[t] = part
    for d in range(1, 8):
        send(lvall.at[t], lvall.at[t], 1, 1, t_peer(d))
    near(3)
    for n in range(4):
        far(n)
    received(qbuf, 0)
    row = pl.ds(2 * z + x % 2, 1)
    use_ref[...] = jnp.where(x // 2 == core, qown[row], qbuf[row]).astype(F32)
    received(lvall.at[pl.ds(0, 7)], 1)
    level = lvall[0]
    for n in range(1, 8):
        level = level + lvall[n]
    add_ref[...] = 0.5 * (level / F + 1e-05)
    loads[2].wait()

    def turn(i, carry):
        @pl.when(i < 4)
        def _():
            own(i + 4)

        @pl.when((i >= 1) & (i < 5))
        def _():
            near(i + 3)

        @pl.when((i >= 2) & (i < 6))
        def _():
            far(i + 2)

        compute(i)
        return carry

    lax.fori_loop(0, 8, turn, 0)

    scale = 1.0 / math.sqrt(F)

    def phases(j):
        left = tile_at(j)
        right = tile_at(j + NOFF)
        a = acc[:HALF, left]
        b = acc[HALF:, right]
        c = acc[HALF:, left]
        d = acc[:HALF, right]
        pos_r = (a - b) * scale
        neg_r = (a + b) * scale
        pos_q = (d + c) * scale
        neg_q = (d - c) * scale
        power = (pos_r * pos_r + pos_q * pos_q) + (neg_r * neg_r + neg_q * neg_q)
        mean = jnp.sum(power, axis=0, keepdims=True) / LAGS
        floor = 0.25 * (mean + 1e-06)

        def halves(value):
            rows = value.reshape(8, 2, 8, TILE)
            return [rows[:, h].reshape(64, TILE) for h in range(2)]

        return floor, ((halves(pos_r), halves(pos_q)), (halves(neg_r), halves(neg_q)))

    def phasors(real, imag, floor):
        depth = jnp.sqrt((real * real + imag * imag) + floor)
        return real, real / depth, imag / depth

    def keep_pair(found, s, k):
        floor, values = found
        for h in range(2):
            pair[h, s, k, :64] = values[s][0][h]
            pair[h, s, k, 64:128] = values[s][1][h]
            pair[h, s, k, 128:] = jnp.broadcast_to(floor, (8, TILE))

    def keep_full(found, s, k):
        floor, values = found
        for h in range(2):
            for part, value in enumerate(phasors(values[s][0][h], values[s][1][h], floor)):
                p[h, s, k, part] = value

    def opened(h, n):
        return phasors(ring[h, n, :64], ring[h, n, 64:128], ring[h, n, 128:129])

    right, left, across = (x + 1) % 4, (x + 3) % 4, (x + 2) % 4

    def across_out(h):
        send(pair.at[h, 0, 0], ring.at[h, 0], 2, 2 + 6 * h, x_peer(1))
        send(pair.at[h, 1, 0], ring.at[h, 1], 2, 3 + 6 * h, x_peer(3))

    def plain_out(h):
        send(pair.at[h, 1, 1], ring.at[h, 2], 2, 4 + 6 * h, x_peer(1))
        send(pair.at[h, 0, 1], ring.at[h, 3], 2, 5 + 6 * h, x_peer(3))

    def both_out(h):
        for s in range(2):
            received(ring.at[h, s], 2 + 6 * h + s)
            for part, value in enumerate(opened(h, s)):
                ringsum[h, s, part] = value + p[h, s, 1, part]
            send(ringsum.at[h, s], ringin.at[h, s], 3, 6 + 6 * h + s, x_peer(3 if s else 1))

    def lag_rows(where):
        return pl.ds(pl.multiple_of(where * 8, 8), 8)

    def z_out(h):
        for s in range(2):
            received(ring.at[h, 3 - s], 5 + 6 * h - s)
            received(ringin.at[h, s], 6 + 6 * h + s)
            for part, value in enumerate(opened(h, 3 - s)):
                zacc[h, s, part] = (p[h, s, 0, part] + value) + ringin[h, s, part]
        for d in (4, 3, 5, 2, 6, 1, 7):
            send(zacc.at[h, :, :, lag_rows((zall + d) % 8)], zbuf.at[h, d - 1], 4 + h, 14 + h, z_peer(d))

    def z_in(h):
        received(zbuf.at[h], 14 + h)
        total = zacc[h, :, :, lag_rows(zall)]
        for d in range(7):
            total = total + zbuf[h, d]
        linear = total[:, 0] / WINDOWS
        real = total[:, 1] / WINDOWS
        imag = total[:, 2] / WINDOWS
        st[h, t] = linear * (real * real + imag * imag)
        for d in range(1, 8):
            send(st.at[h, t], st.at[h, t], 6, 16 + h, t_peer(d))

    found = phases(across)
    keep_pair(found, 0, 0)
    keep_pair(found, 1, 0)
    across_out(0)
    onward = phases(right)
    keep_pair(onward, 1, 1)
    back = phases(left)
    keep_pair(back, 0, 1)
    plain_out(0)
    across_out(1)
    keep_full(onward, 0, 1)
    keep_full(back, 1, 1)
    both_out(0)
    plain_out(1)
    found = phases(x)
    keep_full(found, 0, 0)
    keep_full(found, 1, 0)
    both_out(1)
    z_out(0)
    z_out(1)
    z_in(0)
    z_in(1)

    for h in range(2):
        received(st.at[h, pl.ds(0, 7)], 16 + h)
    shift = off_ref[x]
    whole = shift // 8
    rest = shift % 8 * 16
    wide = lax.broadcasted_iota(jnp.int32, (32, TILE), 1)

    def stack(tile):
        return jnp.concatenate([st[h, tile, s] for s in range(2) for h in range(2)], axis=0)

    pieces = []
    for n in range(4):
        tile = 2 * n + y // 2
        first = tile - whole
        a = jnp.where(first >= 0, stack(jnp.maximum(first, 0)), 0.0)
        b = jnp.where(first >= 1, stack(jnp.maximum(first - 1, 0)), 0.0)
        rev = pltpu.roll(jnp.where(wide < TILE - rest, a, b), rest, 1)
        ahead = stack(tile)
        pieces.append(ahead[:16] + rev[16:])
        pieces.append(ahead[16:] + rev[:16])
    tbuf[...] = jnp.concatenate(pieces, axis=0).T

    def channel_rows(where):
        return pl.ds(pl.multiple_of(y % 2 * 64 + where * 16, 16), 16)

    for d in (1, 2, 3):
        send(tbuf.at[channel_rows((x + d) % 4)], jbuf.at[x], 7, 18, x_peer(d))
    jbuf[x] = tbuf[channel_rows(x)]
    received(jbuf.at[pl.ds(0, 3)], 18)
    group = lax.broadcasted_iota(jnp.int32, (16, TILE), 1) // 32
    for n in range(4):
        merged = jnp.zeros((16, TILE), F32)
        for j in range(NOFF):
            merged = jnp.where(group == j, pltpu.roll(jbuf[j], (32 * (j - n)) % TILE, 1), merged)
        mbuf[n] = merged
    for d in (4, 3, 5, 2, 6, 1, 7):
        send(mbuf.at[(zall + d) % 4], rbuf.at[zall], 8, 19, z_peer(d))
    rbuf[zall] = mbuf[zall % 4]
    received(rbuf.at[pl.ds(0, 7)], 19)
    spot = lax.broadcasted_iota(jnp.int32, (16, TILE), 1)
    span = spot // 16
    for j in range(NOFF):
        for s in range(2):
            merged = jnp.zeros((16, TILE), F32)
            for n in range(8):
                at = 7 - n if s else n
                merged = jnp.where(span == at, pltpu.roll(rbuf[n], (16 * at - 32 * j - 16 * s) % TILE, 1), merged)
            if s:
                for bit in (1, 2, 4, 8):
                    merged = jnp.where(
                        spot // bit % 2 == 1, pltpu.roll(merged, bit, 1), pltpu.roll(merged, TILE - bit, 1)
                    )
            out_ref[1 - s, j] = merged

    gone(lvown, row_sem.at[0])
    gone(g.at[0], own_send.at[0])
    gone(qown, send_sem.at[0])
    gone(lvall.at[pl.ds(0, 7)], send_sem.at[1])
    gone(ring, send_sem.at[2])
    gone(ringin, send_sem.at[3])
    for h in range(2):
        gone(zbuf.at[h], send_sem.at[4 + h])
    gone(st.at[:, pl.ds(0, 7)], send_sem.at[6])
    gone(jbuf.at[pl.ds(0, 3)], send_sem.at[7])
    gone(rbuf.at[pl.ds(0, 7)], send_sem.at[8])
    width = (3, 3, 2, 1)
    for at in range(4):
        ahead, behind = (at + 1) % 4, (at + 3) % 4
        upper = (4, 3, 2, 4)[ahead]
        lower = (4, 4, 3, 2)[behind]

        @pl.when(y == at)
        def _(at=at, ahead=ahead, behind=behind, upper=upper, lower=lower):
            gone(g.at[0, pl.ds(0, upper + width[ahead])], gsend.at[0])
            gone(g.at[0, pl.ds(0, lower + width[behind])], gsend.at[1])
            gone(g.at[0, pl.ds(0, width[ahead] + width[behind])], gsend.at[2])
            gone(g.at[pl.ds(0, width[at])], gsend.at[3])


def whole_window(offsets, spectra, quality, table):
    vmem = pl.BlockSpec(memory_space=pltpu.VMEM)
    return pl.pallas_call(
        window_kernel,
        name="whole_window",
        out_shape=jax.ShapeDtypeStruct((2, NOFF, 16, HALF), F32),
        in_specs=[pl.BlockSpec(memory_space=pltpu.SMEM)] + [pl.BlockSpec(memory_space=pl.ANY)] * 3,
        out_specs=vmem,
        scratch_shapes=[
            pltpu.VMEM((2, 8, FB, NCH), BF),
            pltpu.VMEM((8, NCH), jnp.int32),
            pltpu.VMEM((8, NCH), jnp.int32),
            pltpu.VMEM((8, 2 * HALF, GROUP), BF),
            pltpu.VMEM((8, 8, 4, 2, FB, 256), BF),
            pltpu.VMEM((8, 1, NCH), F32),
            pltpu.VMEM((8, 1, NCH), F32),
            pltpu.VMEM((8, 1, NCH), F32),
            pltpu.VMEM((1, NCH), F32),
            pltpu.VMEM((1, NCH), F32),
            pltpu.VMEM((NEED + 1, 2, 8, FB, TILE), BF),
            pltpu.VMEM((GROUP, 2 * NOFF * TILE), BF),
            pltpu.VMEM((2 * HALF, 2 * NOFF * TILE), F32),
            pltpu.VMEM((2, 2, 2, 3, 64, TILE), F32),
            pltpu.VMEM((2, 2, 2, 136, TILE), F32),
            pltpu.VMEM((2, 4, 136, TILE), F32),
            pltpu.VMEM((2, 2, 3, 64, TILE), F32),
            pltpu.VMEM((2, 2, 3, 64, TILE), F32),
            pltpu.VMEM((2, 2, 3, 64, TILE), F32),
            pltpu.VMEM((2, 7, 2, 3, 8, TILE), F32),
            pltpu.VMEM((2, 8, 2, 8, TILE), F32),
            pltpu.VMEM((TILE, TILE), F32),
            pltpu.VMEM((NOFF, 16, TILE), F32),
            pltpu.VMEM((4, 16, TILE), F32),
            pltpu.VMEM((8, 16, TILE), F32),
            pltpu.SemaphoreType.DMA((3,)),
            pltpu.SemaphoreType.DMA((1,)),
            pltpu.SemaphoreType.DMA((2,)),
            pltpu.SemaphoreType.DMA((4,)),
            pltpu.SemaphoreType.DMA((8, 4, 4)),
            pltpu.SemaphoreType.DMA((8,)),
            pltpu.SemaphoreType.DMA((9,)),
            pltpu.SemaphoreType.DMA((20,)),
        ],
        compiler_params=pltpu.CompilerParams(collective_id=0, has_side_effects=True),
    )(offsets, spectra, quality, table)


def shards(spectra, quality, offsets):
    table = jnp.asarray(half_table()).astype(BF)
    halves = whole_window(offsets, spectra, quality, table)
    return jnp.transpose(halves, (2, 1, 0, 3)).reshape(16, NOFF, LAGS)


def solution(mesh):
    return jax.shard_map(
        shards,
        mesh=mesh,
        in_specs=(P(None, "tm", "chan", None), P("tm", None), P()),
        out_specs=P("chan", None, None),
        check_vma=False,
    )
```
